128 devices in a mesh: rows: 32 (over x, z, core), units: 4 (over y).
Axes of the slice: x: 4, y: 4, z: 4, core: 2. Of those that a mesh axis runs over, the one named last changes fastest.
Arguments:
- residuals: bfloat16 [524288, 2048], P(('rows', 'units')), may hold values from -24 to 24
- loadings: bfloat16 [524288, 256], P(('rows', 'units')), may hold values from -6 to 6
- zero_points: bfloat16 [1024, 2048], P('units'), may hold values from -0.375 to 0.375
- sketch_matrix: bfloat16 [2048, 256], replicated, may hold values from -0.125 to 0.125
- use_lists: int32 [4096, 4], P(('rows', 'units')), may hold values from 0 to 15, all different within a row
Outputs:
- star_basis: float32 [524288, 256], P(('rows', 'units'))
- bin_modes: float32 [2048, 256], P(('rows', 'units'))
The draws below stay inside these ranges and needn't reach their ends.
Inputs may be any that keep to these rules, and one draw needn't show every extreme that they name: `use_lists`: each row names 4 different groups; every group is named by some row.
All inputs are finite; a program needn't handle non-finite values.
Results may differ from the reference program's by a relative error of at most 0.003.
Values may be sent and summed in bfloat16 or wider, within the bound.
No kernel may reach another device: no remote copies, remote signals or barrier semaphores. Data moves between devices by JAX's collectives and lax.ppermute only.
A program may use at most 192 MiB of HBM per device.

```python
from functools import partial
import jax
import jax.numpy as jnp
from jax import lax

NB = 2048
MODES = 256
GROUP = 64
GROUPS = 16
USES = 4
BLOCK_STARS = 128
UNITS = 1024
STARS = 524288
BLOCKS = 4096


def with_spikes(array, rng, source, target, blocks, factor):
    owner, partner = [(jnp.arange(array.shape[position]) // (array.shape[position] // blocks)).reshape([-1 if axis == position else 1 for axis in range(array.ndim)]) for position in (source, target)]
    chosen = jax.random.permutation(rng, blocks)[partner]
    strong = (owner == chosen) | (owner == (partner + blocks // 2) % blocks)
    return jnp.where(strong, factor * array, array)


def block_levels(own_key, shape, split, smallest, top_value):
    gain, own = 1.0, jax.random.fold_in(own_key, 6)
    for axis_at, parts in split:
        draws = jnp.exp(jax.random.uniform(jax.random.fold_in(own, axis_at), (parts,), jnp.float32, smallest / len(split), top_value / len(split)))
        gain = gain * jnp.repeat(draws, shape[axis_at] // parts).reshape([-1 if axis == axis_at else 1 for axis in range(len(shape))])
    return gain


def choose_distinct(key, rows, amount, top, lift):
    sequence = jax.random.permutation(jax.random.fold_in(key, 1), amount)
    favour = sequence
    for power in range(3):
        favour = favour * favour // amount
    favour = favour * lift // amount
    tickets = jax.random.randint(jax.random.fold_in(key, 2), (rows, amount), 0, 4096) + favour
    holders = jax.random.permutation(jax.random.fold_in(key, 3), rows)[jnp.arange(amount) % rows]
    tickets = jnp.where(jnp.arange(rows)[:, None] == holders[None, :], 1 << 14, tickets)
    merit = tickets * amount + jnp.arange(amount)
    return lax.top_k(merit.astype(jnp.int32), top)[1].astype(jnp.int32)


def normal_values(key, extent, deviation, limit, cuts=(), held_as=jnp.bfloat16):
    level = block_levels(key, extent, cuts, -0.22, 0.18) if cuts else 1.0
    entries = jax.random.normal(key, extent, jnp.float32) * deviation * level
    return jnp.minimum(jnp.maximum(entries, -limit), limit).astype(held_as)


def gaussian_with(key, shape, deviation, limit, cuts, heavy, kind=jnp.bfloat16):
    entries = deviation * jax.random.normal(key, shape, jnp.float32)
    if cuts:
        entries = entries * block_levels(key, shape, cuts, -0.22, 0.18)
    return jnp.clip(with_spikes(entries, jax.random.fold_in(key, 3), *heavy), -limit, limit).astype(kind)


def setup_inputs(seed: int = 0) -> dict:
    keys = jax.random.split(jax.random.key(seed), 6)
    return {
        "residuals": gaussian_with(keys[0], (STARS, NB), 1.0, 24.0, ((0, 128),), (0, 1, 128, 5.5)),
        "loadings": normal_values(keys[1], (STARS, USES * GROUP), 1.0, 6.0, ((0, 128),)),
        "zero_points": normal_values(keys[2], (UNITS, NB), (USES * GROUP) ** -0.5, 0.375, ((0, 4),)),
        "sketch_matrix": normal_values(keys[3], (NB, MODES), NB ** -0.5, 0.125),
        "use_lists": choose_distinct(keys[4], BLOCKS, GROUPS, USES, 4096),
    }


def correct_block(tables, pieces):
    res_block, load_block, use_row = pieces
    chosen = tables[use_row].reshape(USES * GROUP, NB)
    offset = jnp.dot(load_block.astype(jnp.float32), chosen.astype(jnp.float32), preferred_element_type=jnp.float32)
    return (res_block.astype(jnp.float32) - offset).astype(jnp.bfloat16)

def reference(residuals, loadings, zero_points, sketch_matrix, use_lists):
    tables = zero_points.reshape(GROUPS, GROUP, NB)
    corrected = lax.map(partial(correct_block, tables), (residuals.reshape(BLOCKS, BLOCK_STARS, NB), loadings.reshape(BLOCKS, BLOCK_STARS, USES * GROUP), use_lists))
    corrected = corrected.reshape(STARS, NB)
    sketched = jnp.dot(corrected.astype(jnp.float32), sketch_matrix.astype(jnp.float32), preferred_element_type=jnp.float32)
    sketch_low = sketched.astype(jnp.bfloat16)
    gram = jnp.dot(sketched.T, sketched, precision=lax.Precision.HIGHEST) / STARS
    lower_factor = jnp.linalg.cholesky(gram)
    star_basis = lax.linalg.triangular_solve(lower_factor, sketched, left_side=False, lower=True, transpose_a=True)
    raw_modes = jnp.dot(corrected.T.astype(jnp.float32), sketch_low.astype(jnp.float32), preferred_element_type=jnp.float32) / STARS
    bin_modes = lax.linalg.triangular_solve(lower_factor, raw_modes, left_side=False, lower=True, transpose_a=True)
    return (star_basis, bin_modes)
```

```python
import functools

import jax
import jax.numpy as jnp
from jax import lax
from jax.experimental import pallas as pl
from jax.experimental.pallas import tpu as pltpu
from jax.sharding import PartitionSpec as P

GROUP = 64
USES = 4
BLOCK_STARS = 128
MODES = 256
STARS = 524288
AXES = ("rows", "units")
F32 = jnp.float32
BF16 = jnp.bfloat16
HIGHEST = lax.Precision.HIGHEST
BIG = pltpu.CompilerParams(vmem_limit_bytes=60 << 20)


def split_low(value):
    high = value.astype(BF16)
    return high, (value - high.astype(F32)).astype(BF16)


def dot_rows(a, b):
    return lax.dot_general(a, b, (((0,), (0,)), ((), ())), preferred_element_type=F32)


def dot_last(a, b, precision=None):
    return lax.dot_general(
        a, b, (((1,), (1,)), ((), ())), preferred_element_type=F32, precision=precision
    )


def permutation(move):
    pairs = []
    for x in range(4):
        for z in range(4):
            for c in range(2):
                for y in range(4):
                    u, w, d, v = move(x, z, c, y)
                    pairs.append((((x * 4 + z) * 2 + c) * 4 + y, ((u * 4 + w) * 2 + d) * 4 + v))
    return pairs


SWAP = permutation(lambda x, z, c, y: (x, z, 1 - c, y))
SHIFTS = {
    "x": [permutation(lambda x, z, c, y, k=k: ((x + k) % 4, z, c, y)) for k in (1, 2, 3)],
    "y": [permutation(lambda x, z, c, y, k=k: (x, z, c, (y + k) % 4)) for k in (1, 2, 3)],
    "z": [permutation(lambda x, z, c, y, k=k: (x, (z + k) % 4, c, y)) for k in (1, 2, 3)],
}


def shift_all(axis, pieces):
    return [lax.ppermute(p, AXES, SHIFTS[axis][k]) for k, p in enumerate(pieces)]


def project_kernel(place, zero_ref, sketch_ref, full_ref, half_ref):
    full_ref[...] = jnp.dot(zero_ref[...], sketch_ref[...], preferred_element_type=F32)
    half = full_ref.shape[0] // 2
    half_ref[...] = full_ref[pl.ds(pl.multiple_of(place[2] * half, half), half), :]


def project(place, zero_points, sketch_matrix):
    units = zero_points.shape[0]
    return pl.pallas_call(
        project_kernel,
        grid_spec=pltpu.PrefetchScalarGridSpec(
            num_scalar_prefetch=1,
            grid=(1,),
            in_specs=[
                pl.BlockSpec(zero_points.shape, lambda i, p: (0, 0)),
                pl.BlockSpec(sketch_matrix.shape, lambda i, p: (0, 0)),
            ],
            out_specs=[
                pl.BlockSpec((units, MODES), lambda i, p: (0, 0)),
                pl.BlockSpec((units // 2, MODES), lambda i, p: (0, 0)),
            ],
        ),
        out_shape=[
            jax.ShapeDtypeStruct((units, MODES), F32),
            jax.ShapeDtypeStruct((units // 2, MODES), F32),
        ],
        name="project",
    )(place, zero_points, sketch_matrix)


def sketch_kernel(res_ref, sketch_ref, out_ref):
    out_ref[...] = jnp.dot(res_ref[...], sketch_ref[...], preferred_element_type=F32)


def sketch(residuals, sketch_matrix, tile=512):
    rows, bins = residuals.shape
    return pl.pallas_call(
        sketch_kernel,
        grid=(rows // tile,),
        in_specs=[
            pl.BlockSpec((tile, bins), lambda i: (i, 0)),
            pl.BlockSpec((bins, MODES), lambda i: (0, 0)),
        ],
        out_specs=pl.BlockSpec((tile, MODES), lambda i: (i, 0)),
        out_shape=jax.ShapeDtypeStruct((rows, MODES), F32),
        cost_estimate=pl.CostEstimate(
            flops=2 * rows * bins * MODES, bytes_accessed=rows * bins * 2 + rows * MODES * 4, transcendentals=0
        ),
        name="sketch",
    )(residuals, sketch_matrix)


def correct_kernel(blocks, place, uses, part_ref, load_ref, own_ref, sw1, sw2, sw3, ha1, ha2, ha3,
                   high_ref, low_ref, gram_keep, gram_send, w_keep, w_send1, w_send2, w_send3,
                   table_high, table_low, gram_hh, gram_hl, weights):
    step = pl.program_id(0)
    units = own_ref.shape[0]
    half = units // 2
    y, c = place[3], place[2]

    @pl.when(step == 0)
    def _():
        gram_hh[...] = jnp.zeros_like(gram_hh)
        gram_hl[...] = jnp.zeros_like(gram_hl)
        weights[...] = jnp.zeros_like(weights)

        def put(start, value):
            high, low = split_low(value)
            rows = pl.ds(pl.multiple_of(start, 128), value.shape[0])
            table_high[rows, :] = high
            table_low[rows, :] = low

        put(y * units, own_ref[...])
        for k, (mine, other) in enumerate(((ha1, sw1), (ha2, sw2), (ha3, sw3))):
            base = lax.rem(y + 3 - k, 4) * units
            put(base + c * half, mine[...])
            put(base + (1 - c) * half, other[...])

    for block in range(blocks):
        rows = pl.ds(block * BLOCK_STARS, BLOCK_STARS)
        groups = [uses[step * blocks + block, use] for use in range(USES)]
        starts = [pl.multiple_of(g * GROUP, GROUP) for g in groups]
        load = load_ref[rows, :]
        high_table = jnp.concatenate([table_high[pl.ds(s, GROUP), :] for s in starts], axis=0)
        low_table = jnp.concatenate([table_low[pl.ds(s, GROUP), :] for s in starts], axis=0)
        offset = jnp.dot(load, high_table, preferred_element_type=F32)
        offset = offset + jnp.dot(load, low_table, preferred_element_type=F32)
        high, low = split_low(part_ref[rows, :] - offset)
        high_ref[rows, :] = high
        low_ref[rows, :] = low
        product = dot_rows(load, high)
        for use in range(USES):
            weights[pl.ds(starts[use], GROUP), :] += product[use * GROUP:(use + 1) * GROUP, :]
    gram_hh[...] += dot_rows(high_ref[...], high_ref[...])
    gram_hl[...] += dot_rows(high_ref[...], low_ref[...])

    @pl.when(step == pl.num_programs(0) - 1)
    def _():
        cross = gram_hl[...]
        gram = gram_hh[...] + cross + cross.T
        packed = jnp.concatenate([gram[:128, :128], gram[128:, :128], gram[128:, 128:]], axis=0)
        gram_hh[...] = gram
        first = c == 0
        gram_keep[...] = jnp.where(first, packed[:192], packed[192:])
        gram_send[...] = jnp.where(first, packed[192:], packed[:192])
        w_keep[...] = weights[pl.ds(pl.multiple_of(y * units, 256), units), :]
        for k, ref in enumerate((w_send1, w_send2, w_send3)):
            base = lax.rem(y + k + 1, 4) * units
            ref[...] = weights[pl.ds(pl.multiple_of(base, 256), units), :].astype(BF16)


def correct(place, use_lists, part, loadings, own, halves, swapped, blocks=4):
    rows = part.shape[0]
    tile = blocks * BLOCK_STARS
    units = own.shape[0]
    whole = lambda i, p, u: (0, 0)
    row = lambda i, p, u: (i, 0)
    return pl.pallas_call(
        functools.partial(correct_kernel, blocks),
        grid_spec=pltpu.PrefetchScalarGridSpec(
            num_scalar_prefetch=2,
            grid=(rows // tile,),
            in_specs=[
                pl.BlockSpec((tile, MODES), row),
                pl.BlockSpec((tile, MODES), row),
                pl.BlockSpec((units, MODES), whole),
            ] + [pl.BlockSpec((units // 2, MODES), whole)] * 6,
            out_specs=[
                pl.BlockSpec((tile, MODES), row),
                pl.BlockSpec((tile, MODES), row),
                pl.BlockSpec((192, 128), whole),
                pl.BlockSpec((192, 128), whole),
            ] + [pl.BlockSpec((units, MODES), whole)] * 4,
            scratch_shapes=[
                pltpu.VMEM((4 * units, MODES), BF16),
                pltpu.VMEM((4 * units, MODES), BF16),
                pltpu.VMEM((MODES, MODES), F32),
                pltpu.VMEM((MODES, MODES), F32),
                pltpu.VMEM((4 * units, MODES), F32),
            ],
        ),
        out_shape=[
            jax.ShapeDtypeStruct((rows, MODES), BF16),
            jax.ShapeDtypeStruct((rows, MODES), BF16),
            jax.ShapeDtypeStruct((192, 128), F32),
            jax.ShapeDtypeStruct((192, 128), F32),
            jax.ShapeDtypeStruct((units, MODES), F32),
        ] + [jax.ShapeDtypeStruct((units, MODES), BF16)] * 3,
        cost_estimate=pl.CostEstimate(
            flops=2 * rows * MODES * MODES * 5, bytes_accessed=rows * MODES * 10, transcendentals=0
        ),
        name="correct",
    )(place, use_lists, part, loadings, own, *swapped, *halves)


def raw_kernel(res_ref, high_ref, out_ref):
    @pl.when(pl.program_id(0) == 0)
    def _():
        out_ref[...] = jnp.zeros_like(out_ref)

    out_ref[...] += dot_rows(high_ref[...], res_ref[...])


def raw_sums(residuals, high, tile=1024):
    rows, bins = residuals.shape
    return pl.pallas_call(
        raw_kernel,
        grid=(rows // tile,),
        in_specs=[
            pl.BlockSpec((tile, bins), lambda i: (i, 0)),
            pl.BlockSpec((tile, MODES), lambda i: (i, 0)),
        ],
        out_specs=pl.BlockSpec((MODES, bins), lambda i: (0, 0)),
        out_shape=jax.ShapeDtypeStruct((MODES, bins), F32),
        cost_estimate=pl.CostEstimate(
            flops=2 * rows * bins * MODES, bytes_accessed=rows * bins * 2 + bins * MODES * 4, transcendentals=0
        ),
        name="raw_sums",
    )(residuals, high)


def finish_kernel(place, raw_ref, zero_ref, w_keep, w1, w2, w3, keep_ref, send_ref, ordered):
    weights = w_keep[...] + w1[...].astype(F32) + w2[...].astype(F32) + w3[...].astype(F32)
    total = raw_ref[...] - dot_rows(weights.astype(BF16), zero_ref[...])
    bins = total.T
    for chip in range(16):
        for pair in range(8):
            source = (chip * 8 + pair) * 16
            target = (pair * 16 + chip) * 16
            ordered[target:target + 16, :] = bins[source:source + 16, :]
    half = keep_ref.shape[0]
    c = place[2]
    keep_ref[...] = ordered[pl.ds(pl.multiple_of(c * half, half), half), :]
    send_ref[...] = ordered[pl.ds(pl.multiple_of((1 - c) * half, half), half), :].astype(BF16)


def finish_raw(place, raw, zero_points, w_keep, w_got):
    bins = raw.shape[1]
    units = zero_points.shape[0]
    whole = lambda i, p: (0, 0)
    return pl.pallas_call(
        finish_kernel,
        grid_spec=pltpu.PrefetchScalarGridSpec(
            num_scalar_prefetch=1,
            grid=(1,),
            in_specs=[
                pl.BlockSpec((MODES, bins), whole),
                pl.BlockSpec((units, bins), whole),
            ] + [pl.BlockSpec((units, MODES), whole)] * 4,
            out_specs=[pl.BlockSpec((bins // 2, MODES), whole)] * 2,
            scratch_shapes=[pltpu.VMEM((bins, MODES), F32)],
        ),
        out_shape=[
            jax.ShapeDtypeStruct((bins // 2, MODES), F32),
            jax.ShapeDtypeStruct((bins // 2, MODES), BF16),
        ],
        cost_estimate=pl.CostEstimate(
            flops=2 * units * bins * MODES, bytes_accessed=bins * MODES * 10, transcendentals=0
        ),
        name="finish_raw",
    )(place, raw, zero_points, w_keep, *w_got)


def quarter_kernel(axis, got_count, place, *refs):
    kept, got = refs[0], refs[1:1 + got_count]
    keep_ref, sends = refs[1 + got_count], refs[2 + got_count:5 + got_count]
    total = refs[5 + got_count]
    value = kept[...]
    for ref in got:
        value = value + ref[...].astype(F32)
    total[...] = value
    rows = keep_ref.shape[0]
    me = place[axis]
    keep_ref[...] = total[pl.ds(pl.multiple_of(me * rows, rows), rows), :]
    for k, ref in enumerate(sends):
        start = lax.rem(me + k + 1, 4) * rows
        ref[...] = total[pl.ds(pl.multiple_of(start, rows), rows), :].astype(ref.dtype)


def quarter(place, axis, kept, got, send_type):
    rows = kept.shape[0] // 4
    whole = lambda i, p: (0, 0)
    out = pl.pallas_call(
        functools.partial(quarter_kernel, axis, len(got)),
        grid_spec=pltpu.PrefetchScalarGridSpec(
            num_scalar_prefetch=1,
            grid=(1,),
            in_specs=[pl.BlockSpec(kept.shape, whole)] * (1 + len(got)),
            out_specs=[pl.BlockSpec((rows, MODES), whole)] * 4,
            scratch_shapes=[pltpu.VMEM(kept.shape, F32)],
        ),
        out_shape=[jax.ShapeDtypeStruct((rows, MODES), F32)]
        + [jax.ShapeDtypeStruct((rows, MODES), send_type)] * 3,
        name="quarter",
    )(place, kept, *got)
    return out[0], out[1:]


def invert_factor(matrix, out_ref, row0):
    lanes = 128
    tiles = 16
    row_in_tile = lax.broadcasted_iota(jnp.int32, (8, lanes), 0)
    rows = lax.broadcasted_iota(jnp.int32, (lanes, lanes), 0)
    cols = lax.broadcasted_iota(jnp.int32, (lanes, lanes), 1)
    unit = (rows == cols).astype(F32)
    work = [matrix[8 * i:8 * i + 8, :] for i in range(tiles)]
    inverse = [unit[8 * i:8 * i + 8, :] for i in range(tiles)]

    def spread(value):
        return jnp.broadcast_to(value, (8, lanes))

    for j in range(0, lanes, 2):
        tile, at = divmod(j, 8)
        r1, r2 = work[tile][at:at + 1, :], work[tile][at + 1:at + 2, :]
        x1, x2 = inverse[tile][at:at + 1, :], inverse[tile][at + 1:at + 2, :]
        a = jnp.broadcast_to(r1[:, j:j + 1], (1, lanes))
        b = jnp.broadcast_to(r1[:, j + 1:j + 2], (1, lanes))
        d = jnp.broadcast_to(r2[:, j + 1:j + 2], (1, lanes))
        det = a * d - b * b
        scale = 1.0 / det
        t1, t2 = spread((d * r1 - b * r2) * scale), spread((a * r2 - b * r1) * scale)
        u1, u2 = spread((d * x1 - b * x2) * scale), spread((a * x2 - b * x1) * scale)
        root = lax.rsqrt(a)
        out_ref[row0 + j:row0 + j + 1, :] = x1 * root
        out_ref[row0 + j + 1:row0 + j + 2, :] = (a * x2 - b * x1) * (root * lax.rsqrt(det))
        for i in range(tile, tiles):
            if i == tile:
                if at == 6:
                    continue
                below = row_in_tile > at + 1
                m1 = jnp.where(below, spread(work[i][:, j:j + 1]), 0.0)
                m2 = jnp.where(below, spread(work[i][:, j + 1:j + 2]), 0.0)
            else:
                m1, m2 = spread(work[i][:, j:j + 1]), spread(work[i][:, j + 1:j + 2])
            work[i] = work[i] - (m1 * t1 + m2 * t2)
            inverse[i] = inverse[i] - (m1 * u1 + m2 * u2)


def dot_plain(a, b):
    return jnp.dot(a, b, preferred_element_type=F32, precision=HIGHEST)


def basis_kernel(place, mine_ref, other_ref, high_ref, low_ref, out_ref, inverse_ref, top, bottom, inv_high, inv_low):
    @pl.when(pl.program_id(0) == 0)
    def _():
        first = place[2] == 0
        mine, other = mine_ref[...] * (1.0 / STARS), other_ref[...] * (1.0 / STARS)
        packed = jnp.concatenate(
            [jnp.where(first, mine, other), jnp.where(first, other, mine)], axis=0
        )
        invert_factor(packed[:128], top, 0)
        upper = top[...]
        lower = dot_last(packed[128:256], upper, HIGHEST)
        invert_factor(packed[256:] - dot_last(lower, lower, HIGHEST), bottom, 0)
        corner = bottom[...]
        left = -dot_plain(corner, dot_plain(lower, upper))
        inverse_ref[:128, :128] = upper
        inverse_ref[:128, 128:] = jnp.zeros_like(upper)
        inverse_ref[128:, :128] = left
        inverse_ref[128:, 128:] = corner
        high, low = split_low(inverse_ref[...])
        inv_high[...] = high
        inv_low[...] = low

    out_ref[...] = (
        dot_last(high_ref[...], inv_high[...])
        + dot_last(high_ref[...], inv_low[...])
        + dot_last(low_ref[...], inv_high[...])
    )


def basis(place, mine, other, high, low, tile=512):
    rows = high.shape[0]
    whole = lambda i, p: (0, 0)
    row = lambda i, p: (i, 0)
    return pl.pallas_call(
        basis_kernel,
        grid_spec=pltpu.PrefetchScalarGridSpec(
            num_scalar_prefetch=1,
            grid=(rows // tile,),
            in_specs=[
                pl.BlockSpec((192, 128), whole),
                pl.BlockSpec((192, 128), whole),
                pl.BlockSpec((tile, MODES), row),
                pl.BlockSpec((tile, MODES), row),
            ],
            out_specs=[
                pl.BlockSpec((tile, MODES), row),
                pl.BlockSpec((MODES, MODES), whole),
            ],
            scratch_shapes=[
                pltpu.VMEM((128, 128), F32),
                pltpu.VMEM((128, 128), F32),
                pltpu.VMEM((MODES, MODES), BF16),
                pltpu.VMEM((MODES, MODES), BF16),
            ],
        ),
        out_shape=[
            jax.ShapeDtypeStruct((rows, MODES), F32),
            jax.ShapeDtypeStruct((MODES, MODES), F32),
        ],
        cost_estimate=pl.CostEstimate(
            flops=2 * rows * MODES * MODES * 3 + (1 << 34), bytes_accessed=rows * MODES * 8, transcendentals=0
        ),
        name="basis",
    )(place, mine, other, high, low)


def modes_kernel(kept, got1, got2, got3, inverse_ref, out_ref):
    raw = (kept[...] + got1[...] + got2[...] + got3[...]) * (1.0 / STARS)
    out_ref[...] = dot_last(raw, inverse_ref[...], HIGHEST)


def modes(kept, got, inverse):
    return pl.pallas_call(
        modes_kernel,
        out_shape=jax.ShapeDtypeStruct(kept.shape, F32),
        name="modes",
    )(kept, *got, inverse)


def on_device(residuals, loadings, zero_points, sketch_matrix, use_lists):
    r = lax.axis_index("rows")
    y = lax.axis_index("units")
    place = jnp.stack([r // 8, (r // 2) % 4, r % 2, y]).astype(jnp.int32)
    own, half = project(place, zero_points, sketch_matrix)
    halves = shift_all("y", [half] * 3)
    swapped = [lax.ppermute(h, AXES, SWAP) for h in halves]
    part = sketch(residuals, sketch_matrix)
    high, low, gram_keep, gram_send, w_keep, *w_sends = correct(
        place, use_lists, part, loadings, own, halves, swapped
    )
    gram = gram_keep + lax.ppermute(gram_send, AXES, SWAP)
    w_got = shift_all("y", w_sends)
    raw = raw_sums(residuals, high)
    for axis in "yxz":
        one, two, three = shift_all(axis, [gram] * 3)
        gram = (gram + two) + (one + three)
    other = lax.ppermute(gram, AXES, SWAP)
    keep, send = finish_raw(place, raw, zero_points, w_keep, w_got)
    keep, sends = quarter(place, 3, keep, [lax.ppermute(send, AXES, SWAP)], BF16)
    keep, sends = quarter(place, 0, keep, shift_all("y", sends), F32)
    keep, sends = quarter(place, 1, keep, shift_all("x", sends), F32)
    got = shift_all("z", sends)
    star_basis, inverse = basis(place, gram, other, high, low)
    bin_modes = modes(keep, got, inverse)
    return (star_basis, bin_modes)


def solution(mesh):
    in_specs = (
        P(("rows", "units"), None),
        P(("rows", "units"), None),
        P("units", None),
        P(),
        P(("rows", "units"), None),
    )
    out_specs = (P(("rows", "units"), None), P(("rows", "units"), None))
    return jax.shard_map(
        on_device, mesh=mesh, in_specs=in_specs, out_specs=out_specs, check_vma=False
    )
```

```python
import functools

import jax
import jax.numpy as jnp
from jax import lax
from jax.experimental import pallas as pl
from jax.experimental.pallas import tpu as pltpu
from jax.sharding import PartitionSpec as P

GROUP = 64
USES = 4
BLOCK_STARS = 128
MODES = 256
STARS = 524288
AXES = ("rows", "units")
F32 = jnp.float32
BF16 = jnp.bfloat16
HIGHEST = lax.Precision.HIGHEST


def split_low(value):
    high = value.astype(BF16)
    return high, (value - high.astype(F32)).astype(BF16)


def dot_rows(a, b):
    return lax.dot_general(a, b, (((0,), (0,)), ((), ())), preferred_element_type=F32)


def dot_last(a, b, precision=None):
    return lax.dot_general(
        a, b, (((1,), (1,)), ((), ())), preferred_element_type=F32, precision=precision
    )


def permutation(move):
    pairs = []
    for x in range(4):
        for z in range(4):
            for c in range(2):
                for y in range(4):
                    u, w, d, v = move(x, z, c, y)
                    pairs.append((((x * 4 + z) * 2 + c) * 4 + y, ((u * 4 + w) * 2 + d) * 4 + v))
    return pairs


SWAP = permutation(lambda x, z, c, y: (x, z, 1 - c, y))
SHIFTS = {
    "x": [permutation(lambda x, z, c, y, k=k: ((x + k) % 4, z, c, y)) for k in (1, 2, 3)],
    "y": [permutation(lambda x, z, c, y, k=k: (x, z, c, (y + k) % 4)) for k in (1, 2, 3)],
    "z": [permutation(lambda x, z, c, y, k=k: (x, (z + k) % 4, c, y)) for k in (1, 2, 3)],
}


def shift_all(axis, pieces):
    return [lax.ppermute(p, AXES, SHIFTS[axis][k]) for k, p in enumerate(pieces)]


def on_chip(shape, kind=F32):
    return pltpu.VMEM(shape, kind)


def resident(kernel, name, scalars, arrays, outs, scratch=(), flops=0, limit=16, out_specs=None):
    vmem = pl.BlockSpec(memory_space=pltpu.VMEM)
    smem = pl.BlockSpec(memory_space=pltpu.SMEM)
    arrays = [pltpu.with_memory_space_constraint(a, pltpu.VMEM) for a in arrays]
    return pl.pallas_call(
        kernel,
        in_specs=[smem] * len(scalars) + [vmem] * len(arrays),
        out_specs=out_specs or [vmem] * len(outs),
        out_shape=list(outs),
        scratch_shapes=list(scratch),
        compiler_params=pltpu.CompilerParams(vmem_limit_bytes=limit << 20),
        cost_estimate=pl.CostEstimate(flops=flops, bytes_accessed=1 << 16, transcendentals=0),
        name=name,
    )(*scalars, *arrays)


def project_kernel(place, zero_ref, sketch_ref, full_ref, half_ref):
    full_ref[...] = jnp.dot(zero_ref[...], sketch_ref[...], preferred_element_type=F32)
    half = full_ref.shape[0] // 2
    half_ref[...] = full_ref[pl.ds(pl.multiple_of(place[2] * half, half), half), :]


def sketch_kernel(tile, res_ref, sketch_ref, out_ref):
    def body(i, carry):
        rows = pl.ds(pl.multiple_of(i * tile, tile), tile)
        out_ref[rows, :] = jnp.dot(res_ref[rows, :], sketch_ref[...], preferred_element_type=F32)
        return carry

    lax.fori_loop(0, res_ref.shape[0] // tile, body, 0)


def correct_kernel(blocks, place, uses, part_ref, load_ref, own_ref, half_ref, other_ref,
                   high_ref, low_ref, gram_keep, gram_send, w_keep, w_send1, w_send2, w_send3,
                   table_high, table_low, gram_hh, gram_hl, weights):
    units = own_ref.shape[0]
    half = units // 2
    tile = blocks * BLOCK_STARS
    y, c = place[3], place[2]
    gram_hh[...] = jnp.zeros_like(gram_hh)
    gram_hl[...] = jnp.zeros_like(gram_hl)
    weights[...] = jnp.zeros_like(weights)

    def put(start, value):
        high, low = split_low(value)
        rows = pl.ds(pl.multiple_of(start, 128), value.shape[0])
        table_high[rows, :] = high
        table_low[rows, :] = low

    put(y * units, own_ref[...])
    for k in range(3):
        base = lax.rem(y + 3 - k, 4) * units
        put(base + c * half, half_ref[k * half:(k + 1) * half, :])
        put(base + (1 - c) * half, other_ref[k * half:(k + 1) * half, :])

    def step(i, carry):
        for block in range(blocks):
            rows = pl.ds(pl.multiple_of(i * tile + block * BLOCK_STARS, BLOCK_STARS), BLOCK_STARS)
            groups = [uses[use, i * blocks + block] for use in range(USES)]
            starts = [pl.multiple_of(g * GROUP, GROUP) for g in groups]
            load = load_ref[rows, :]
            high_table = jnp.concatenate([table_high[pl.ds(s, GROUP), :] for s in starts], axis=0)
            low_table = jnp.concatenate([table_low[pl.ds(s, GROUP), :] for s in starts], axis=0)
            offset = jnp.dot(load, high_table, preferred_element_type=F32)
            offset = offset + jnp.dot(load, low_table, preferred_element_type=F32)
            high, low = split_low(part_ref[rows, :] - offset)
            high_ref[rows, :] = high
            low_ref[rows, :] = low
            product = dot_rows(load, high)
            for use in range(USES):
                weights[pl.ds(starts[use], GROUP), :] += product[use * GROUP:(use + 1) * GROUP, :]
        rows = pl.ds(pl.multiple_of(i * tile, tile), tile)
        gram_hh[...] += dot_rows(high_ref[rows, :], high_ref[rows, :])
        gram_hl[...] += dot_rows(high_ref[rows, :], low_ref[rows, :])
        return carry

    lax.fori_loop(0, part_ref.shape[0] // tile, step, 0)
    cross = gram_hl[...]
    gram = gram_hh[...] + cross + cross.T
    packed = jnp.concatenate([gram[:128, :128], gram[128:, :128], gram[128:, 128:]], axis=0)
    zero = jnp.concatenate([packed[:96], packed[96:192]], axis=1)
    one = jnp.concatenate([packed[192:288], packed[288:]], axis=1)
    first = c == 0
    gram_keep[...] = jnp.where(first, zero, one)
    gram_send[...] = jnp.where(first, one, zero)
    w_keep[...] = weights[pl.ds(pl.multiple_of(y * units, 256), units), :]
    for k, ref in enumerate((w_send1, w_send2, w_send3)):
        base = lax.rem(y + k + 1, 4) * units
        ref[...] = weights[pl.ds(pl.multiple_of(base, 256), units), :].astype(BF16)


def raw_kernel(tile, res_ref, high_ref, out_ref):
    def body(i, carry):
        columns = pl.ds(pl.multiple_of(i * tile, tile), tile)
        out_ref[:, columns] = dot_rows(high_ref[...], res_ref[:, columns])
        return carry

    lax.fori_loop(0, res_ref.shape[1] // tile, body, 0)


def finish_kernel(place, raw_ref, zero_ref, w_keep, w1, w2, w3, keep_ref, send_ref, ordered):
    weights = w_keep[...] + w1[...].astype(F32) + w2[...].astype(F32) + w3[...].astype(F32)
    total = raw_ref[...] - dot_rows(weights.astype(BF16), zero_ref[...])
    bins = total.T
    for chip in range(16):
        for pair in range(8):
            source = (chip * 8 + pair) * 16
            target = (pair * 16 + chip) * 16
            ordered[target:target + 16, :] = bins[source:source + 16, :]
    half = keep_ref.shape[0]
    c = place[2]
    keep_ref[...] = ordered[pl.ds(pl.multiple_of(c * half, half), half), :]
    send_ref[...] = ordered[pl.ds(pl.multiple_of((1 - c) * half, half), half), :].astype(BF16)


def quarters(me, total, kind):
    rows = total.shape[0] // 4
    pieces = [
        lax.dynamic_slice_in_dim(total, lax.rem(me + k, 4) * rows, rows, 0) for k in range(4)
    ]
    return pieces[0], [p.astype(kind) for p in pieces[1:]]


def add_four(own, got):
    return (own + got[1]) + (got[0] + got[2])


def invert_factor(matrix, out_ref, row0):
    lanes = 128
    tiles = 16
    row_in_tile = lax.broadcasted_iota(jnp.int32, (8, lanes), 0)
    rows = lax.broadcasted_iota(jnp.int32, (lanes, lanes), 0)
    cols = lax.broadcasted_iota(jnp.int32, (lanes, lanes), 1)
    unit = (rows == cols).astype(F32)
    work = [matrix[8 * i:8 * i + 8, :] for i in range(tiles)]
    inverse = [unit[8 * i:8 * i + 8, :] for i in range(tiles)]

    def spread(value):
        return jnp.broadcast_to(value, (8, lanes))

    for j in range(0, lanes, 2):
        tile, at = divmod(j, 8)
        r1, r2 = work[tile][at:at + 1, :], work[tile][at + 1:at + 2, :]
        x1, x2 = inverse[tile][at:at + 1, :], inverse[tile][at + 1:at + 2, :]
        a = jnp.broadcast_to(r1[:, j:j + 1], (1, lanes))
        b = jnp.broadcast_to(r1[:, j + 1:j + 2], (1, lanes))
        d = jnp.broadcast_to(r2[:, j + 1:j + 2], (1, lanes))
        det = a * d - b * b
        scale = 1.0 / det
        t1, t2 = spread((d * r1 - b * r2) * scale), spread((a * r2 - b * r1) * scale)
        u1, u2 = spread((d * x1 - b * x2) * scale), spread((a * x2 - b * x1) * scale)
        root = lax.rsqrt(a)
        out_ref[row0 + j:row0 + j + 1, :] = x1 * root
        out_ref[row0 + j + 1:row0 + j + 2, :] = (a * x2 - b * x1) * (root * lax.rsqrt(det))
        for i in range(tile, tiles):
            if i == tile:
                if at == 6:
                    continue
                below = row_in_tile > at + 1
                m1 = jnp.where(below, spread(work[i][:, j:j + 1]), 0.0)
                m2 = jnp.where(below, spread(work[i][:, j + 1:j + 2]), 0.0)
            else:
                m1, m2 = spread(work[i][:, j:j + 1]), spread(work[i][:, j + 1:j + 2])
            work[i] = work[i] - (m1 * t1 + m2 * t2)
            inverse[i] = inverse[i] - (m1 * u1 + m2 * u2)


def dot_plain(a, b):
    return jnp.dot(a, b, preferred_element_type=F32, precision=HIGHEST)

def dot_plain(a, b):
    return jnp.dot(a, b, preferred_element_type=F32, precision=HIGHEST)


def factor_kernel(place, mine_ref, other_ref, inverse_ref, inv_high, inv_low, top, bottom):
    first = place[2] == 0
    mine, other = mine_ref[...] * (1.0 / STARS), other_ref[...] * (1.0 / STARS)
    zero, one = jnp.where(first, mine, other), jnp.where(first, other, mine)
    packed = jnp.concatenate([zero[:, :128], zero[:, 128:], one[:, :128], one[:, 128:]], axis=0)
    invert_factor(packed[:128], top, 0)
    upper = top[...]
    lower = dot_last(packed[128:256], upper, HIGHEST)
    invert_factor(packed[256:] - dot_last(lower, lower, HIGHEST), bottom, 0)
    corner = bottom[...]
    left = -dot_plain(corner, dot_plain(lower, upper))
    inverse_ref[:128, :128] = upper
    inverse_ref[:128, 128:] = jnp.zeros_like(upper)
    inverse_ref[128:, :128] = left
    inverse_ref[128:, 128:] = corner
    high, low = split_low(inverse_ref[...])
    inv_high[...] = high
    inv_low[...] = low


def basis_kernel(tiles, high_ref, low_ref, inv_high, inv_low, out_ref, buffer, sems):
    tile = high_ref.shape[0] // tiles
    copies = []
    for i in range(tiles):
        rows = pl.ds(i * tile, tile)
        buffer[rows, :] = (
            dot_last(high_ref[rows, :], inv_high[...])
            + dot_last(high_ref[rows, :], inv_low[...])
            + dot_last(low_ref[rows, :], inv_high[...])
        )
        copy = pltpu.make_async_copy(buffer.at[rows, :], out_ref.at[rows, :], sems.at[i])
        copy.start()
        copies.append(copy)
    for copy in copies:
        copy.wait()


def modes_kernel(kept, got1, got2, got3, inverse_ref, out_ref):
    raw = (kept[...] + got1[...] + got2[...] + got3[...]) * (1.0 / STARS)
    out_ref[...] = dot_last(raw, inverse_ref[...], HIGHEST)


def on_device(residuals, loadings, zero_points, sketch_matrix, use_lists):
    rows, bins = residuals.shape
    units = zero_points.shape[0]
    r = lax.axis_index("rows")
    x, z, c, y = r // 8, (r // 2) % 4, r % 2, lax.axis_index("units")
    place = jnp.stack([x, z, c, y]).astype(jnp.int32)
    square = (MODES, MODES)
    own, half = resident(
        project_kernel, "project", [place], [zero_points, sketch_matrix],
        [on_chip((units, MODES)), on_chip((units // 2, MODES))], flops=2 * units * bins * MODES,
    )
    halves = jnp.concatenate(shift_all("y", [half] * 3), axis=0)
    others = lax.ppermute(halves, AXES, SWAP)
    part, = resident(
        functools.partial(sketch_kernel, 1024), "sketch", [], [residuals, sketch_matrix],
        [on_chip((rows, MODES))], flops=2 * rows * bins * MODES,
    )
    high, low, gram_keep, gram_send, w_keep, *w_sends = resident(
        functools.partial(correct_kernel, 4), "correct", [place, use_lists.T],
        [part, loadings, own, halves, others],
        [on_chip((rows, MODES), BF16)] * 2 + [on_chip((96, MODES))] * 2 + [on_chip((units, MODES))]
        + [on_chip((units, MODES), BF16)] * 3,
        [
            pltpu.VMEM((4 * units, MODES), BF16),
            pltpu.VMEM((4 * units, MODES), BF16),
            pltpu.VMEM(square, F32),
            pltpu.VMEM(square, F32),
            pltpu.VMEM((4 * units, MODES), F32),
        ],
        flops=2 * rows * bins * MODES,
    )
    gram_high, gram_low = split_low(gram_keep + lax.ppermute(gram_send, AXES, SWAP))
    raw, = resident(
        functools.partial(raw_kernel, 512), "raw_sums", [], [residuals, high],
        [on_chip((MODES, bins))], flops=2 * rows * bins * MODES,
    )
    got = shift_all("y", [jnp.concatenate([w, gram_high, gram_low], axis=0) for w in w_sends])
    join = lambda h, l: h.astype(F32) + l.astype(F32)
    gram = add_four(join(gram_high, gram_low), [join(g[units:units + 96], g[units + 96:]) for g in got])
    for axis in "xz":
        gram = add_four(gram, shift_all(axis, [gram] * 3))
    gram_other = lax.ppermute(gram, AXES, SWAP)
    keep, send = resident(
        finish_kernel, "finish_raw", [place], [raw, zero_points, w_keep] + [g[:units] for g in got],
        [on_chip((bins // 2, MODES)), on_chip((bins // 2, MODES), BF16)],
        [pltpu.VMEM((bins, MODES), F32)], flops=2 * units * bins * MODES,
    )
    total = keep + lax.ppermute(send, AXES, SWAP).astype(F32)
    keep, sends = quarters(y, total, BF16)
    keep, sends = quarters(x, add_four(keep, [g.astype(F32) for g in shift_all("y", sends)]), F32)
    keep, sends = quarters(z, add_four(keep, shift_all("x", sends)), F32)
    raw_got = shift_all("z", sends)
    inverse, inv_high, inv_low = resident(
        factor_kernel, "factor", [place], [gram, gram_other],
        [on_chip(square), on_chip(square, BF16), on_chip(square, BF16)],
        [pltpu.VMEM((128, 128), F32)] * 2, flops=1 << 33,
    )
    star_basis, = resident(
        functools.partial(basis_kernel, 4), "basis", [], [high, low, inv_high, inv_low],
        [jax.ShapeDtypeStruct((rows, MODES), F32)],
        [pltpu.VMEM((rows, MODES), F32), pltpu.SemaphoreType.DMA((4,))],
        flops=6 * rows * MODES * MODES, out_specs=[pl.BlockSpec(memory_space=pl.ANY)],
    )
    bin_modes, = resident(
        modes_kernel, "modes", [], [keep, *raw_got, inverse],
        [jax.ShapeDtypeStruct((keep.shape[0], MODES), F32)], flops=1 << 28,
    )
    return (star_basis, bin_modes)


def solution(mesh):
    in_specs = (
        P(("rows", "units"), None),
        P(("rows", "units"), None),
        P("units", None),
        P(),
        P(("rows", "units"), None),
    )
    out_specs = (P(("rows", "units"), None), P(("rows", "units"), None))
    return jax.shard_map(
        on_device, mesh=mesh, in_specs=in_specs, out_specs=out_specs, check_vma=False
    )
```

```python
import functools

import jax
import jax.numpy as jnp
from jax import lax
from jax.experimental import pallas as pl
from jax.experimental.pallas import tpu as pltpu
from jax.sharding import PartitionSpec as P

GROUP = 64
USES = 4
BLOCK_STARS = 128
MODES = 256
STARS = 524288
AXES = ("rows", "units")
F32 = jnp.float32
BF16 = jnp.bfloat16
HIGHEST = lax.Precision.HIGHEST


def split_low(value):
    high = value.astype(BF16)
    return high, (value - high.astype(F32)).astype(BF16)


def dot_rows(a, b):
    return lax.dot_general(a, b, (((0,), (0,)), ((), ())), preferred_element_type=F32)


def dot_last(a, b, precision=None):
    return lax.dot_general(
        a, b, (((1,), (1,)), ((), ())), preferred_element_type=F32, precision=precision
    )


def permutation(move):
    pairs = []
    for x in range(4):
        for z in range(4):
            for c in range(2):
                for y in range(4):
                    u, w, d, v = move(x, z, c, y)
                    pairs.append((((x * 4 + z) * 2 + c) * 4 + y, ((u * 4 + w) * 2 + d) * 4 + v))
    return pairs


SWAP = permutation(lambda x, z, c, y: (x, z, 1 - c, y))
SHIFTS = {
    "x": [permutation(lambda x, z, c, y, k=k: ((x + k) % 4, z, c, y)) for k in (1, 2, 3)],
    "y": [permutation(lambda x, z, c, y, k=k: (x, z, c, (y + k) % 4)) for k in (1, 2, 3)],
    "z": [permutation(lambda x, z, c, y, k=k: (x, (z + k) % 4, c, y)) for k in (1, 2, 3)],
}


def shift_all(axis, pieces):
    return [lax.ppermute(p, AXES, SHIFTS[axis][k]) for k, p in enumerate(pieces)]


def on_chip(shape, kind=F32):
    return pltpu.VMEM(shape, kind)


def resident(kernel, name, scalars, arrays, outs, scratch=(), flops=0, limit=16, out_specs=None, far=()):
    vmem = pl.BlockSpec(memory_space=pltpu.VMEM)
    smem = pl.BlockSpec(memory_space=pltpu.SMEM)
    arrays = [pltpu.with_memory_space_constraint(a, pltpu.VMEM) for a in arrays]
    far = [pltpu.with_memory_space_constraint(a, pltpu.HBM) for a in far]
    return pl.pallas_call(
        kernel,
        in_specs=[smem] * len(scalars) + [vmem] * len(arrays) + [pl.BlockSpec(memory_space=pltpu.HBM)] * len(far),
        out_specs=out_specs or [vmem] * len(outs),
        out_shape=list(outs),
        scratch_shapes=list(scratch),
        compiler_params=pltpu.CompilerParams(vmem_limit_bytes=limit << 20),
        cost_estimate=pl.CostEstimate(flops=flops, bytes_accessed=1 << 16, transcendentals=0),
        name=name,
    )(*scalars, *arrays, *far)


def project_kernel(place, zero_hbm, sketch_hbm, full_ref, half_ref, zero, sketch, sems):
    copies = [
        pltpu.make_async_copy(zero_hbm, zero, sems.at[0]),
        pltpu.make_async_copy(sketch_hbm, sketch, sems.at[1]),
    ]
    for copy in copies:
        copy.start()
    for copy in copies:
        copy.wait()
    full_ref[...] = jnp.dot(zero[...], sketch[...], preferred_element_type=F32)
    half = full_ref.shape[0] // 2
    half_ref[...] = full_ref[pl.ds(pl.multiple_of(place[2] * half, half), half), :]


def sketch_kernel(tiles, sketch_ref, res_hbm, out_ref, res_ref, flag_ref, sems):
    tile = res_ref.shape[0] // tiles
    copies = []
    for i in range(tiles):
        rows = pl.ds(i * tile, tile)
        copies.append(pltpu.make_async_copy(res_hbm.at[rows, :], res_ref.at[rows, :], sems.at[i]))
        copies[i].start()
    for i in range(tiles):
        copies[i].wait()
        rows = pl.ds(i * tile, tile)
        out_ref[rows, :] = jnp.dot(res_ref[rows, :], sketch_ref[...], preferred_element_type=F32)
    flag_ref[...] = jnp.zeros_like(flag_ref)


def correct_kernel(blocks, place, uses, part_ref, load_ref, own_ref, half_ref, other_ref,
                   high_ref, low_ref, gram_keep, gram_send, w_keep, w_send1, w_send2, w_send3,
                   table_high, table_low, gram_hh, gram_hl, weights):
    units = own_ref.shape[0]
    half = units // 2
    tile = blocks * BLOCK_STARS
    y, c = place[3], place[2]
    gram_hh[...] = jnp.zeros_like(gram_hh)
    gram_hl[...] = jnp.zeros_like(gram_hl)
    weights[...] = jnp.zeros_like(weights)

    def put(start, value):
        high, low = split_low(value)
        rows = pl.ds(pl.multiple_of(start, 128), value.shape[0])
        table_high[rows, :] = high
        table_low[rows, :] = low

    put(y * units, own_ref[...])
    for k in range(3):
        base = lax.rem(y + 3 - k, 4) * units
        put(base + c * half, half_ref[k * half:(k + 1) * half, :])
        put(base + (1 - c) * half, other_ref[k * half:(k + 1) * half, :])

    def step(i, carry):
        for block in range(blocks):
            rows = pl.ds(pl.multiple_of(i * tile + block * BLOCK_STARS, BLOCK_STARS), BLOCK_STARS)
            groups = [uses[use, i * blocks + block] for use in range(USES)]
            starts = [pl.multiple_of(g * GROUP, GROUP) for g in groups]
            load = load_ref[rows, :]
            high_table = jnp.concatenate([table_high[pl.ds(s, GROUP), :] for s in starts], axis=0)
            low_table = jnp.concatenate([table_low[pl.ds(s, GROUP), :] for s in starts], axis=0)
            offset = jnp.dot(load, high_table, preferred_element_type=F32)
            offset = offset + jnp.dot(load, low_table, preferred_element_type=F32)
            high, low = split_low(part_ref[rows, :] - offset)
            high_ref[rows, :] = high
            low_ref[rows, :] = low
            product = dot_rows(load, high)
            for use in range(USES):
                weights[pl.ds(starts[use], GROUP), :] += product[use * GROUP:(use + 1) * GROUP, :]
        rows = pl.ds(pl.multiple_of(i * tile, tile), tile)
        gram_hh[...] += dot_rows(high_ref[rows, :], high_ref[rows, :])
        gram_hl[...] += dot_rows(high_ref[rows, :], low_ref[rows, :])
        return carry

    lax.fori_loop(0, part_ref.shape[0] // tile, step, 0)
    cross = gram_hl[...]
    gram = gram_hh[...] + cross + cross.T
    packed = jnp.concatenate([gram[:128, :128], gram[128:, :128], gram[128:, 128:]], axis=0)
    zero = jnp.concatenate([packed[:96], packed[96:192]], axis=1)
    one = jnp.concatenate([packed[192:288], packed[288:]], axis=1)
    first = c == 0
    gram_keep[...] = jnp.where(first, zero, one)
    gram_send[...] = jnp.where(first, one, zero)
    w_keep[...] = weights[pl.ds(pl.multiple_of(y * units, 256), units), :]
    for k, ref in enumerate((w_send1, w_send2, w_send3)):
        base = lax.rem(y + k + 1, 4) * units
        ref[...] = weights[pl.ds(pl.multiple_of(base, 256), units), :].astype(BF16)


def raw_kernel(tile, res_ref, high_ref, out_ref):
    def body(i, carry):
        columns = pl.ds(pl.multiple_of(i * tile, tile), tile)
        out_ref[:, columns] = dot_rows(high_ref[...], res_ref[:, columns])
        return carry

    lax.fori_loop(0, res_ref.shape[1] // tile, body, 0)


def finish_kernel(place, raw_ref, zero_ref, w_keep, w1, w2, w3, keep_ref, send_ref, ordered):
    weights = w_keep[...] + w1[...].astype(F32) + w2[...].astype(F32) + w3[...].astype(F32)
    total = raw_ref[...] - dot_rows(weights.astype(BF16), zero_ref[...])
    bins = total.T
    for chip in range(16):
        for core in range(2):
            source = (chip * 2 + core) * 64
            target = (core * 16 + chip) * 64
            ordered[target:target + 64, :] = bins[source:source + 64, :]
    half = keep_ref.shape[0]
    c = place[2]
    keep_ref[...] = ordered[pl.ds(pl.multiple_of(c * half, half), half), :]
    send_ref[...] = ordered[pl.ds(pl.multiple_of((1 - c) * half, half), half), :].astype(BF16)


def quarters(me, total, kind):
    rows = total.shape[0] // 4
    pieces = [
        lax.dynamic_slice_in_dim(total, lax.rem(me + k, 4) * rows, rows, 0) for k in range(4)
    ]
    return pieces[0], [p.astype(kind) for p in pieces[1:]]


def add_four(own, got):
    return (own + got[1]) + (got[0] + got[2])


def invert_factor(matrix, out_ref, panel=8):
    lanes, tiles = 128, 16
    row_in_tile = lax.broadcasted_iota(jnp.int32, (8, lanes), 0)
    rows = lax.broadcasted_iota(jnp.int32, (lanes, lanes), 0)
    unit = (rows == lax.broadcasted_iota(jnp.int32, (lanes, lanes), 1)).astype(F32)
    work = [matrix[8 * i:8 * i + 8, :] for i in range(tiles)]
    inverse = [unit[8 * i:8 * i + 8, :] for i in range(tiles)]

    def spread(value):
        return jnp.broadcast_to(value, (8, lanes))

    for j in range(0, lanes, panel):
        tile, at = divmod(j, 8)
        top = [spread(work[tile][at + k:at + k + 1, :]) for k in range(panel)]
        low = [spread(inverse[tile][at + k:at + k + 1, :]) for k in range(panel)]
        entry = {
            (p, q): spread(top[p][:, j + q:j + q + 1])
            for p in range(panel) for q in range(p, panel)
        }
        top_solved, low_solved, factors = {}, {}, {}
        for k in range(0, panel, 2):
            a, b, d = entry[k, k], entry[k, k + 1], entry[k + 1, k + 1]
            det = a * d - b * b
            scale = 1.0 / det
            i00, i01, i11 = d * scale, b * scale, a * scale
            root = lax.rsqrt(a)
            r = at + k
            out_ref[j + k:j + k + 1, :] = (low[k] * root)[r:r + 1, :]
            under = (a * low[k + 1] - b * low[k]) * (root * lax.rsqrt(det))
            out_ref[j + k + 1:j + k + 2, :] = under[r + 1:r + 2, :]
            for rows_of, solved in ((top, top_solved), (low, low_solved)):
                solved[k] = i00 * rows_of[k] - i01 * rows_of[k + 1]
                solved[k + 1] = i11 * rows_of[k + 1] - i01 * rows_of[k]
            for q in range(k + 2, panel):
                u, v = entry[k, q], entry[k + 1, q]
                factors[k, q], factors[k + 1, q] = i00 * u - i01 * v, i11 * v - i01 * u
            for p in range(k + 2, panel):
                for q in range(p, panel):
                    entry[p, q] = entry[p, q] - (entry[k, p] * factors[k, q] + entry[k + 1, p] * factors[k + 1, q])
                for rows_of in (top, low):
                    rows_of[p] = rows_of[p] - (factors[k, p] * rows_of[k] + factors[k + 1, p] * rows_of[k + 1])
        for solved in (top_solved, low_solved):
            for k in range(panel - 3, -1, -1):
                for q in range(panel - 1, k // 2 * 2 + 1, -1):
                    solved[k] = solved[k] - factors[k, q] * solved[q]
        top_rows = [top_solved[k] for k in range(panel)]
        low_rows = [low_solved[k] for k in range(panel)]
        for i in range(tile, tiles):
            if i == tile and at + panel == 8:
                continue
            columns = [spread(work[i][:, j + k:j + k + 1]) for k in range(panel)]
            if i == tile:
                columns = [jnp.where(row_in_tile >= at + panel, m, 0.0) for m in columns]
            work[i] = work[i] - sum_pairs([m * t for m, t in zip(columns, top_rows)])
            inverse[i] = inverse[i] - sum_pairs([m * t for m, t in zip(columns, low_rows)])


def sum_pairs(terms):
    while len(terms) > 1:
        terms = [a + b for a, b in zip(terms[::2], terms[1::2])]
    return terms[0]


def dot_plain(a, b):
    return jnp.dot(a, b, preferred_element_type=F32, precision=HIGHEST)

def dot_plain(a, b):
    return jnp.dot(a, b, preferred_element_type=F32, precision=HIGHEST)


def factor_kernel(place, mine_ref, other_ref, inverse_ref, inv_high, inv_low, top, bottom):
    first = place[2] == 0
    mine, other = mine_ref[...] * (1.0 / STARS), other_ref[...] * (1.0 / STARS)
    zero, one = jnp.where(first, mine, other), jnp.where(first, other, mine)
    packed = jnp.concatenate([zero[:, :128], zero[:, 128:], one[:, :128], one[:, 128:]], axis=0)
    invert_factor(packed[:128], top)
    upper = top[...]
    lower = dot_last(packed[128:256], upper, HIGHEST)
    invert_factor(packed[256:] - dot_last(lower, lower, HIGHEST), bottom)
    corner = bottom[...]
    left = -dot_plain(corner, dot_plain(lower, upper))
    inverse_ref[:128, :128] = upper
    inverse_ref[:128, 128:] = jnp.zeros_like(upper)
    inverse_ref[128:, :128] = left
    inverse_ref[128:, 128:] = corner
    high, low = split_low(inverse_ref[...])
    inv_high[...] = high
    inv_low[...] = low


def basis_kernel(tiles, high_ref, low_ref, inv_high, inv_low, out_ref, buffer, sems):
    tile = high_ref.shape[0] // tiles
    copies = []
    for i in range(tiles):
        rows = pl.ds(i * tile, tile)
        buffer[rows, :] = (
            dot_last(high_ref[rows, :], inv_high[...])
            + dot_last(high_ref[rows, :], inv_low[...])
            + dot_last(low_ref[rows, :], inv_high[...])
        )
        copy = pltpu.make_async_copy(buffer.at[rows, :], out_ref.at[rows, :], sems.at[i])
        copy.start()
        copies.append(copy)
    for copy in copies:
        copy.wait()


def modes_kernel(kept, got1, got2, got3, inverse_ref, out_ref):
    raw = (kept[...] + got1[...] + got2[...] + got3[...]) * (1.0 / STARS)
    out_ref[...] = dot_last(raw, inverse_ref[...], HIGHEST)


def on_device(residuals, loadings, zero_points, sketch_matrix, use_lists):
    rows, bins = residuals.shape
    units = zero_points.shape[0]
    r = lax.axis_index("rows")
    x, z, c, y = r // 8, (r // 2) % 4, r % 2, lax.axis_index("units")
    place = jnp.stack([x, z, c, y]).astype(jnp.int32)
    square = (MODES, MODES)
    own, half = resident(
        project_kernel, "project", [place], [],
        [on_chip((units, MODES)), on_chip((units // 2, MODES))],
        [
            pltpu.VMEM((units, bins), BF16),
            pltpu.VMEM((bins, MODES), BF16),
            pltpu.SemaphoreType.DMA((2,)),
        ],
        flops=2 * units * bins * MODES, far=[zero_points, sketch_matrix],
    )
    shifted = shift_all("y", [half] * 3)
    part, residuals, flag = resident(
        functools.partial(sketch_kernel, 8), "sketch", [], [sketch_matrix],
        [on_chip((rows, MODES)), on_chip((rows, bins), BF16), jax.ShapeDtypeStruct((8, 128), F32)],
        [pltpu.SemaphoreType.DMA((8,))], flops=2 * rows * bins * MODES, far=[residuals],
    )
    halves = jnp.concatenate(shifted, axis=0) + flag[0, 0]
    others = lax.ppermute(halves, AXES, SWAP)
    high, low, gram_keep, gram_send, w_keep, *w_sends = resident(
        functools.partial(correct_kernel, 4), "correct", [place, use_lists.T],
        [part, loadings, own, halves, others],
        [on_chip((rows, MODES), BF16)] * 2 + [on_chip((96, MODES))] * 2 + [on_chip((units, MODES))]
        + [on_chip((units, MODES), BF16)] * 3,
        [
            pltpu.VMEM((4 * units, MODES), BF16),
            pltpu.VMEM((4 * units, MODES), BF16),
            pltpu.VMEM(square, F32),
            pltpu.VMEM(square, F32),
            pltpu.VMEM((4 * units, MODES), F32),
        ],
        flops=2 * rows * bins * MODES,
    )
    w_got = shift_all("y", w_sends)
    gram = gram_keep + lax.ppermute(gram_send, AXES, SWAP)
    raw, = resident(
        functools.partial(raw_kernel, 512), "raw_sums", [], [residuals, high],
        [on_chip((MODES, bins))], flops=2 * rows * bins * MODES,
    )
    for axis in "xzy":
        gram = add_four(gram, shift_all(axis, [gram] * 3))
    gram_other = lax.ppermute(gram, AXES, SWAP)
    keep, send = resident(
        finish_kernel, "finish_raw", [place], [raw, zero_points, w_keep, *w_got],
        [on_chip((bins // 2, MODES)), on_chip((bins // 2, MODES), BF16)],
        [pltpu.VMEM((bins, MODES), F32)], flops=2 * units * bins * MODES,
    )
    total = keep + lax.ppermute(send, AXES, SWAP).astype(F32)
    keep, sends = quarters(x, total, BF16)
    keep, sends = quarters(z, add_four(keep, [g.astype(F32) for g in shift_all("x", sends)]), F32)
    keep, sends = quarters(y, add_four(keep, shift_all("z", sends)), F32)
    raw_got = shift_all("y", sends)
    inverse, inv_high, inv_low = resident(
        factor_kernel, "factor", [place], [gram, gram_other],
        [on_chip(square), on_chip(square, BF16), on_chip(square, BF16)],
        [pltpu.VMEM((128, 128), F32)] * 2, flops=1 << 33,
    )
    star_basis, = resident(
        functools.partial(basis_kernel, 4), "basis", [], [high, low, inv_high, inv_low],
        [jax.ShapeDtypeStruct((rows, MODES), F32)],
        [pltpu.VMEM((rows, MODES), F32), pltpu.SemaphoreType.DMA((4,))],
        flops=6 * rows * MODES * MODES, out_specs=[pl.BlockSpec(memory_space=pltpu.HBM)],
    )
    bin_modes, = resident(
        modes_kernel, "modes", [], [keep, *raw_got, inverse],
        [jax.ShapeDtypeStruct((keep.shape[0], MODES), F32)], flops=1 << 28,
    )
    return (star_basis, bin_modes)


def solution(mesh):
    in_specs = (
        P(("rows", "units"), None),
        P(("rows", "units"), None),
        P("units", None),
        P(),
        P(("rows", "units"), None),
    )
    out_specs = (P(("rows", "units"), None), P(("rows", "units"), None))
    return jax.shard_map(
        on_device, mesh=mesh, in_specs=in_specs, out_specs=out_specs, check_vma=False
    )
```

```python
import functools

import jax
import jax.numpy as jnp
from jax import lax
from jax.experimental import pallas as pl
from jax.experimental.pallas import tpu as pltpu
from jax.sharding import PartitionSpec as P


GROUP = 64
USES = 4
BLOCK_STARS = 128
MODES = 256
STARS = 524288
AXES = ("rows", "units")
DEPTH = 2
F32 = jnp.float32
BF16 = jnp.bfloat16
HIGHEST = lax.Precision.HIGHEST


def split_low(value):
    high = value.astype(BF16)
    return high, (value - high.astype(F32)).astype(BF16)


def dot_rows(a, b):
    return lax.dot_general(a, b, (((0,), (0,)), ((), ())), preferred_element_type=F32)


def dot_last(a, b, precision=None):
    return lax.dot_general(
        a, b, (((1,), (1,)), ((), ())), preferred_element_type=F32, precision=precision
    )


def permutation(move):
    pairs = []
    for x in range(4):
        for z in range(4):
            for c in range(2):
                for y in range(4):
                    u, w, d, v = move(x, z, c, y)
                    pairs.append((((x * 4 + z) * 2 + c) * 4 + y, ((u * 4 + w) * 2 + d) * 4 + v))
    return pairs


SWAP = permutation(lambda x, z, c, y: (x, z, 1 - c, y))
SHIFTS = {
    "x": [permutation(lambda x, z, c, y, k=k: ((x + k) % 4, z, c, y)) for k in (1, 2, 3)],
    "y": [permutation(lambda x, z, c, y, k=k: (x, z, c, (y + k) % 4)) for k in (1, 2, 3)],
    "z": [permutation(lambda x, z, c, y, k=k: (x, (z + k) % 4, c, y)) for k in (1, 2, 3)],
}

PAIRS = {
    "x": [permutation(lambda x, z, c, y: (x ^ 1, z, c, y)), permutation(lambda x, z, c, y: (3 - x, z, c, y))],
    "y": [permutation(lambda x, z, c, y: (x, z, c, y ^ 1)), permutation(lambda x, z, c, y: (x, z, c, 3 - y))],
    "z": [permutation(lambda x, z, c, y: (x, z ^ 1, c, y)), permutation(lambda x, z, c, y: (x, 3 - z, c, y))],
}


def send(value, pairs):
    return lax.ppermute(value, AXES, pairs)


def shift_all(axis, pieces):
    return [send(p, SHIFTS[axis][k]) for k, p in enumerate(pieces)]


def on_chip(shape, kind=F32):
    return pltpu.VMEM(shape, kind)


def resident(kernel, scalars, arrays, outs, scratch=(), flops=0, limit=16, out_specs=None, far=()):
    vmem = pl.BlockSpec(memory_space=pltpu.VMEM)
    smem = pl.BlockSpec(memory_space=pltpu.SMEM)
    arrays = [pltpu.with_memory_space_constraint(a, pltpu.VMEM) for a in arrays]
    far = [pltpu.with_memory_space_constraint(a, pltpu.HBM) for a in far]
    return pl.pallas_call(
        kernel,
        in_specs=[smem] * len(scalars) + [vmem] * len(arrays) + [pl.BlockSpec(memory_space=pltpu.HBM)] * len(far),
        out_specs=out_specs or [vmem] * len(outs),
        out_shape=list(outs),
        scratch_shapes=list(scratch),
        compiler_params=pltpu.CompilerParams(vmem_limit_bytes=limit << 20),
        cost_estimate=pl.CostEstimate(flops=flops, bytes_accessed=1 << 16, transcendentals=0),
    )(*scalars, *arrays, *far)


def project_kernel(place, zero_hbm, sketch_hbm, full_ref, half_ref, sketch, zero, sems):
    copies = [
        pltpu.make_async_copy(zero_hbm, zero, sems.at[0]),
        pltpu.make_async_copy(sketch_hbm, sketch, sems.at[1]),
    ]
    for copy in copies:
        copy.start()
    for copy in copies:
        copy.wait()
    full_ref[...] = jnp.dot(zero[...], sketch[...], preferred_element_type=F32)
    half = full_ref.shape[0] // 2
    half_ref[...] = full_ref[pl.ds(pl.multiple_of(place[2] * half, half), half), :]


def sketch_kernel(tiles, sketch_ref, res_hbm, out_ref, res_ref, flag_ref, sems):
    tile = res_ref.shape[0] // tiles
    copies = []
    for i in range(tiles):
        rows = pl.ds(i * tile, tile)
        copies.append(pltpu.make_async_copy(res_hbm.at[rows, :], res_ref.at[rows, :], sems.at[i]))
    for i in range(DEPTH):
        copies[i].start()
    for i in range(tiles):
        copies[i].wait()
        if i + DEPTH < tiles:
            copies[i + DEPTH].start()
        rows = pl.ds(i * tile, tile)
        out_ref[rows, :] = jnp.dot(res_ref[rows, :], sketch_ref[...], preferred_element_type=F32)
    flag_ref[...] = jnp.zeros_like(flag_ref)


def correct_kernel(blocks, place, uses, part_ref, load_ref, own_ref, half_ref, other_ref,
                   high_ref, low_ref, gram_keep, gram_send, w_keep, w_send1, w_send2, w_send3,
                   table_high, table_low, gram_hh, gram_hl, weights):
    units = own_ref.shape[0]
    half = units // 2
    tile = blocks * BLOCK_STARS
    y, c = place[3], place[2]
    gram_hh[...] = jnp.zeros_like(gram_hh)
    gram_hl[...] = jnp.zeros_like(gram_hl)
    weights[...] = jnp.zeros_like(weights)

    def put(start, value):
        high, low = split_low(value)
        rows = pl.ds(pl.multiple_of(start, 128), value.shape[0])
        table_high[rows, :] = high
        table_low[rows, :] = low

    put(y * units, own_ref[...])
    for k in range(3):
        base = lax.rem(y + 3 - k, 4) * units
        put(base + c * half, half_ref[k * half:(k + 1) * half, :])
        put(base + (1 - c) * half, other_ref[k * half:(k + 1) * half, :])

    def step(i, carry):
        for block in range(blocks):
            rows = pl.ds(pl.multiple_of(i * tile + block * BLOCK_STARS, BLOCK_STARS), BLOCK_STARS)
            groups = [uses[use, i * blocks + block] for use in range(USES)]
            starts = [pl.multiple_of(g * GROUP, GROUP) for g in groups]
            load = load_ref[rows, :]
            high_table = jnp.concatenate([table_high[pl.ds(s, GROUP), :] for s in starts], axis=0)
            low_table = jnp.concatenate([table_low[pl.ds(s, GROUP), :] for s in starts], axis=0)
            offset = jnp.dot(load, high_table, preferred_element_type=F32)
            offset = offset + jnp.dot(load, low_table, preferred_element_type=F32)
            high, low = split_low(part_ref[rows, :] - offset)
            high_ref[rows, :] = high
            low_ref[rows, :] = low
            product = dot_rows(load, high)
            for use in range(USES):
                weights[pl.ds(starts[use], GROUP), :] += product[use * GROUP:(use + 1) * GROUP, :]
        rows = pl.ds(pl.multiple_of(i * tile, tile), tile)
        gram_hh[...] += dot_rows(high_ref[rows, :], high_ref[rows, :])
        gram_hl[...] += dot_rows(high_ref[rows, :], low_ref[rows, :])
        return carry

    lax.fori_loop(0, part_ref.shape[0] // tile, step, 0)
    cross = gram_hl[...]
    gram = gram_hh[...] + cross + cross.T
    packed = jnp.concatenate([gram[:128, :128], gram[128:, :128], gram[128:, 128:]], axis=0)
    zero = jnp.concatenate([packed[:96], packed[96:192]], axis=1)
    one = jnp.concatenate([packed[192:288], packed[288:]], axis=1)
    first = c == 0
    gram_keep[...] = jnp.where(first, zero, one)
    gram_send[...] = jnp.where(first, one, zero)
    w_keep[...] = weights[pl.ds(pl.multiple_of(y * units, 256), units), :]
    for k, ref in enumerate((w_send1, w_send2, w_send3)):
        base = lax.rem(y + k + 1, 4) * units
        ref[...] = weights[pl.ds(pl.multiple_of(base, 256), units), :].astype(BF16)


def raw_kernel(tile, res_ref, high_ref, out_ref):
    def body(i, carry):
        columns = pl.ds(pl.multiple_of(i * tile, tile), tile)
        out_ref[:, columns] = dot_rows(high_ref[...], res_ref[:, columns])
        return carry

    lax.fori_loop(0, res_ref.shape[1] // tile, body, 0)


def finish_kernel(place, raw_ref, zero_ref, w_keep, w1, w2, w3, keep_ref, send_ref, ordered):
    weights = w_keep[...] + w1[...].astype(F32) + w2[...].astype(F32) + w3[...].astype(F32)
    total = raw_ref[...] - dot_rows(weights.astype(BF16), zero_ref[...])
    bins = total.T
    for chip in range(16):
        for core in range(2):
            source = (chip * 2 + core) * 64
            target = (core * 16 + chip) * 64
            ordered[target:target + 64, :] = bins[source:source + 64, :]
    half = keep_ref.shape[0]
    c = place[2]
    keep_ref[...] = ordered[pl.ds(pl.multiple_of(c * half, half), half), :]
    send_ref[...] = ordered[pl.ds(pl.multiple_of((1 - c) * half, half), half), :].astype(BF16)


def quarters(me, total, kind):
    rows = total.shape[0] // 4
    pieces = [
        lax.dynamic_slice_in_dim(total, lax.rem(me + k, 4) * rows, rows, 0) for k in range(4)
    ]
    return pieces[0], [p.astype(kind) for p in pieces[1:]]


def add_four(own, got):
    return (own + got[1]) + (got[0] + got[2])


def invert_factor(matrix, out_ref, panel=8):
    lanes, tiles = 128, 16
    row_in_tile = lax.broadcasted_iota(jnp.int32, (8, lanes), 0)
    rows = lax.broadcasted_iota(jnp.int32, (lanes, lanes), 0)
    unit = (rows == lax.broadcasted_iota(jnp.int32, (lanes, lanes), 1)).astype(F32)
    work = [matrix[8 * i:8 * i + 8, :] for i in range(tiles)]
    inverse = [unit[8 * i:8 * i + 8, :] for i in range(tiles)]

    def spread(value):
        return jnp.broadcast_to(value, (8, lanes))

    for j in range(0, lanes, panel):
        tile, at = divmod(j, 8)
        top = [spread(work[tile][at + k:at + k + 1, :]) for k in range(panel)]
        low = [spread(inverse[tile][at + k:at + k + 1, :]) for k in range(panel)]
        entry = {
            (p, q): spread(top[p][:, j + q:j + q + 1])
            for p in range(panel) for q in range(p, panel)
        }
        top_solved, low_solved, factors = {}, {}, {}
        for k in range(0, panel, 2):
            a, b, d = entry[k, k], entry[k, k + 1], entry[k + 1, k + 1]
            det = a * d - b * b
            scale = 1.0 / det
            i00, i01, i11 = d * scale, b * scale, a * scale
            root = lax.rsqrt(a)
            r = at + k
            out_ref[j + k:j + k + 1, :] = (low[k] * root)[r:r + 1, :]
            under = (a * low[k + 1] - b * low[k]) * (root * lax.rsqrt(det))
            out_ref[j + k + 1:j + k + 2, :] = under[r + 1:r + 2, :]
            for rows_of, solved in ((top, top_solved), (low, low_solved)):
                solved[k] = i00 * rows_of[k] - i01 * rows_of[k + 1]
                solved[k + 1] = i11 * rows_of[k + 1] - i01 * rows_of[k]
            for q in range(k + 2, panel):
                u, v = entry[k, q], entry[k + 1, q]
                factors[k, q], factors[k + 1, q] = i00 * u - i01 * v, i11 * v - i01 * u
            for p in range(k + 2, panel):
                for q in range(p, panel):
                    entry[p, q] = entry[p, q] - (entry[k, p] * factors[k, q] + entry[k + 1, p] * factors[k + 1, q])
                for rows_of in (top, low):
                    rows_of[p] = rows_of[p] - (factors[k, p] * rows_of[k] + factors[k + 1, p] * rows_of[k + 1])
        for solved in (top_solved, low_solved):
            for k in range(panel - 3, -1, -1):
                for q in range(panel - 1, k // 2 * 2 + 1, -1):
                    solved[k] = solved[k] - factors[k, q] * solved[q]
        top_rows = [top_solved[k] for k in range(panel)]
        low_rows = [low_solved[k] for k in range(panel)]
        for i in range(tile, tiles):
            if i == tile and at + panel == 8:
                continue
            columns = [spread(work[i][:, j + k:j + k + 1]) for k in range(panel)]
            if i == tile:
                columns = [jnp.where(row_in_tile >= at + panel, m, 0.0) for m in columns]
            work[i] = work[i] - sum_pairs([m * t for m, t in zip(columns, top_rows)])
            inverse[i] = inverse[i] - sum_pairs([m * t for m, t in zip(columns, low_rows)])


def sum_pairs(terms):
    while len(terms) > 1:
        terms = [a + b for a, b in zip(terms[::2], terms[1::2])]
    return terms[0]


def dot_plain(a, b):
    return jnp.dot(a, b, preferred_element_type=F32, precision=HIGHEST)


def dot_plain(a, b):
    return jnp.dot(a, b, preferred_element_type=F32, precision=HIGHEST)


def factor_kernel(place, mine_ref, other_ref, inverse_ref, inv_high, inv_low, top, bottom):
    first = place[2] == 0
    mine, other = mine_ref[...] * (1.0 / STARS), other_ref[...] * (1.0 / STARS)
    zero, one = jnp.where(first, mine, other), jnp.where(first, other, mine)
    packed = jnp.concatenate([zero[:, :128], zero[:, 128:], one[:, :128], one[:, 128:]], axis=0)
    invert_factor(packed[:128], top)
    upper = top[...]
    lower = dot_last(packed[128:256], upper, HIGHEST)
    invert_factor(packed[256:] - dot_last(lower, lower, HIGHEST), bottom)
    corner = bottom[...]
    left = -dot_plain(corner, dot_plain(lower, upper))
    inverse_ref[:128, :128] = upper
    inverse_ref[:128, 128:] = jnp.zeros_like(upper)
    inverse_ref[128:, :128] = left
    inverse_ref[128:, 128:] = corner
    high, low = split_low(inverse_ref[...])
    inv_high[...] = high
    inv_low[...] = low


def basis_kernel(tiles, high_ref, low_ref, inv_high, inv_low, out_ref, buffer, sems):
    tile = high_ref.shape[0] // tiles
    copies = []
    for i in range(tiles):
        rows = pl.ds(i * tile, tile)
        buffer[rows, :] = (
            dot_last(high_ref[rows, :], inv_high[...])
            + dot_last(high_ref[rows, :], inv_low[...])
            + dot_last(low_ref[rows, :], inv_high[...])
        )
        copy = pltpu.make_async_copy(buffer.at[rows, :], out_ref.at[rows, :], sems.at[i])
        copy.start()
        copies.append(copy)
    for copy in copies:
        copy.wait()


def modes_kernel(kept, got1, got2, got3, inverse_ref, out_ref):
    raw = (kept[...] + got1[...] + got2[...] + got3[...]) * (1.0 / STARS)
    out_ref[...] = dot_last(raw, inverse_ref[...], HIGHEST)


def on_device(residuals, loadings, zero_points, sketch_matrix, use_lists):
    rows, bins = residuals.shape
    units = zero_points.shape[0]
    r = lax.axis_index("rows")
    x, z, c, y = r // 8, (r // 2) % 4, r % 2, lax.axis_index("units")
    place = jnp.stack([x, z, c, y]).astype(jnp.int32)
    square = (MODES, MODES)
    own, half, sketch_near = resident(
        project_kernel, [place], [],
        [on_chip((units, MODES)), on_chip((units // 2, MODES)), on_chip((bins, MODES), BF16)],
        [pltpu.VMEM((units, bins), BF16), pltpu.SemaphoreType.DMA((2,))],
        flops=2 * units * bins * MODES, far=[zero_points, sketch_matrix],
    )
    shifted = shift_all("y", [half] * 3)
    part, residuals, flag = resident(
        functools.partial(sketch_kernel, 8), [], [sketch_near],
        [on_chip((rows, MODES)), on_chip((rows, bins), BF16), on_chip((8, 128))],
        [pltpu.SemaphoreType.DMA((8,))], flops=2 * rows * bins * MODES, far=[residuals],
    )
    halves = jnp.concatenate(shifted, axis=0) + flag[0, 0]
    others = send(halves, SWAP)
    high, low, gram_keep, gram_send, w_keep, *w_sends = resident(
        functools.partial(correct_kernel, 4), [place, use_lists.T],
        [part, loadings, own, halves, others],
        [on_chip((rows, MODES), BF16)] * 2 + [on_chip((96, MODES))] * 2 + [on_chip((units, MODES))]
        + [on_chip((units, MODES), BF16)] * 3,
        [
            pltpu.VMEM((4 * units, MODES), BF16),
            pltpu.VMEM((4 * units, MODES), BF16),
            pltpu.VMEM(square, F32),
            pltpu.VMEM(square, F32),
            pltpu.VMEM((4 * units, MODES), F32),
        ],
        flops=2 * rows * bins * MODES,
    )
    w_got = shift_all("y", w_sends)
    gram = gram_keep + send(gram_send, SWAP)
    raw, = resident(
        functools.partial(raw_kernel, 512), [], [residuals, high],
        [on_chip((MODES, bins))], flops=2 * rows * bins * MODES,
    )
    for axis in "xzy":
        for pairs in PAIRS[axis]:
            gram = gram + send(gram, pairs)
    gram_other = send(gram, SWAP)
    keep, sent = resident(
        finish_kernel, [place], [raw, zero_points, w_keep, *w_got],
        [on_chip((bins // 2, MODES)), on_chip((bins // 2, MODES), BF16)],
        [pltpu.VMEM((bins, MODES), F32)], flops=2 * units * bins * MODES,
    )
    arrived = send(sent, SWAP)
    keep, sends = quarters(x, keep + arrived.astype(F32), BF16)
    keep, sends = quarters(z, add_four(keep, [g.astype(F32) for g in shift_all("x", sends)]), F32)
    keep, sends = quarters(y, add_four(keep, shift_all("z", sends)), F32)
    raw_got = shift_all("y", sends)
    inverse, inv_high, inv_low = resident(
        factor_kernel, [place], [gram, gram_other],
        [on_chip(square), on_chip(square, BF16), on_chip(square, BF16)],
        [pltpu.VMEM((128, 128), F32)] * 2, flops=1 << 33,
    )
    star_basis, = resident(
        functools.partial(basis_kernel, 4), [], [high, low, inv_high, inv_low],
        [jax.ShapeDtypeStruct((rows, MODES), F32)],
        [pltpu.VMEM((rows, MODES), F32), pltpu.SemaphoreType.DMA((4,))],
        flops=6 * rows * MODES * MODES, out_specs=[pl.BlockSpec(memory_space=pltpu.HBM)],
    )
    bin_modes, = resident(
        modes_kernel, [], [keep, *raw_got, inverse],
        [jax.ShapeDtypeStruct((keep.shape[0], MODES), F32)], flops=1 << 28,
    )
    return (star_basis, bin_modes)


def solution(mesh):
    in_specs = (
        P(("rows", "units"), None),
        P(("rows", "units"), None),
        P("units", None),
        P(),
        P(("rows", "units"), None),
    )
    out_specs = (P(("rows", "units"), None), P(("rows", "units"), None))
    return jax.shard_map(on_device, mesh=mesh, in_specs=in_specs, out_specs=out_specs, check_vma=False)
```

```python
import functools

import jax
import jax.numpy as jnp
from jax import lax
from jax.experimental import pallas as pl
from jax.experimental.pallas import tpu as pltpu
from jax.sharding import PartitionSpec as P


GROUP = 64
USES = 4
BLOCK_STARS = 128
MODES = 256
STARS = 524288
AXES = ("rows", "units")
F32 = jnp.float32
BF16 = jnp.bfloat16
HIGHEST = lax.Precision.HIGHEST


def split_low(value):
    high = value.astype(BF16)
    return high, (value - high.astype(F32)).astype(BF16)


def dot_rows(a, b):
    return lax.dot_general(a, b, (((0,), (0,)), ((), ())), preferred_element_type=F32)


def dot_last(a, b, precision=None):
    return lax.dot_general(
        a, b, (((1,), (1,)), ((), ())), preferred_element_type=F32, precision=precision
    )


def permutation(move):
    pairs = []
    for x in range(4):
        for z in range(4):
            for c in range(2):
                for y in range(4):
                    u, w, d, v = move(x, z, c, y)
                    pairs.append((((x * 4 + z) * 2 + c) * 4 + y, ((u * 4 + w) * 2 + d) * 4 + v))
    return pairs


SWAP = permutation(lambda x, z, c, y: (x, z, 1 - c, y))
SHIFTS = {
    "x": [permutation(lambda x, z, c, y, k=k: ((x + k) % 4, z, c, y)) for k in (1, 2, 3)],
    "y": [permutation(lambda x, z, c, y, k=k: (x, z, c, (y + k) % 4)) for k in (1, 2, 3)],
    "z": [permutation(lambda x, z, c, y, k=k: (x, (z + k) % 4, c, y)) for k in (1, 2, 3)],
}

PAIRS = {
    "x": [permutation(lambda x, z, c, y: (x ^ 1, z, c, y)), permutation(lambda x, z, c, y: (3 - x, z, c, y))],
    "y": [permutation(lambda x, z, c, y: (x, z, c, y ^ 1)), permutation(lambda x, z, c, y: (x, z, c, 3 - y))],
    "z": [permutation(lambda x, z, c, y: (x, z ^ 1, c, y)), permutation(lambda x, z, c, y: (x, 3 - z, c, y))],
}


def send(value, pairs):
    return lax.ppermute(value, AXES, pairs)


def shift_all(axis, pieces):
    return [send(p, SHIFTS[axis][k]) for k, p in enumerate(pieces)]


def on_chip(shape, kind=F32):
    return pltpu.VMEM(shape, kind)


def resident(kernel, scalars, arrays, outs, scratch=(), flops=0, limit=16, out_specs=None, far=()):
    vmem = pl.BlockSpec(memory_space=pltpu.VMEM)
    smem = pl.BlockSpec(memory_space=pltpu.SMEM)
    arrays = [pltpu.with_memory_space_constraint(a, pltpu.VMEM) for a in arrays]
    far = [pltpu.with_memory_space_constraint(a, pltpu.HBM) for a in far]
    return pl.pallas_call(
        kernel,
        in_specs=[smem] * len(scalars) + [vmem] * len(arrays) + [pl.BlockSpec(memory_space=pltpu.HBM)] * len(far),
        out_specs=out_specs or [vmem] * len(outs),
        out_shape=list(outs),
        scratch_shapes=list(scratch),
        compiler_params=pltpu.CompilerParams(vmem_limit_bytes=limit << 20),
        cost_estimate=pl.CostEstimate(flops=flops, bytes_accessed=1 << 16, transcendentals=0),
    )(*scalars, *arrays, *far)


def project_kernel(place, zero_hbm, sketch_hbm, full_ref, half_ref, sketch, zero, sems):
    copies = [
        pltpu.make_async_copy(zero_hbm, zero, sems.at[0]),
        pltpu.make_async_copy(sketch_hbm, sketch, sems.at[1]),
    ]
    for copy in copies:
        copy.start()
    for copy in copies:
        copy.wait()
    full_ref[...] = jnp.dot(zero[...], sketch[...], preferred_element_type=F32)
    half = full_ref.shape[0] // 2
    half_ref[...] = full_ref[pl.ds(pl.multiple_of(place[2] * half, half), half), :]


def fetch_kernel(sketch_ref, res_hbm, out_ref, res_ref, sems):
    half = out_ref.shape[0]
    copies = []
    for i in range(2):
        rows = pl.ds(i * half, half)
        copies.append(pltpu.make_async_copy(res_hbm.at[rows, :], res_ref.at[rows, :], sems.at[i]))
        copies[i].start()
    copies[0].wait()
    sketch_kernel(sketch_ref, res_ref, out_ref, 0)
    copies[1].wait()


def sketch_kernel(sketch_ref, res_ref, out_ref, first):
    tile = out_ref.shape[0] // 2
    for i in range(2):
        rows = pl.ds(i * tile, tile)
        out_ref[rows, :] = jnp.dot(
            res_ref[pl.ds(first + i * tile, tile), :], sketch_ref[...], preferred_element_type=F32
        )


def sketch_rest_kernel(sketch_ref, res_ref, out_ref):
    sketch_kernel(sketch_ref, res_ref, out_ref, res_ref.shape[0] // 2)


def correct_kernel(place, uses, part_a, part_b, load_ref, own_ref, half_ref, other_ref,
                   high_ref, low_ref, gram_keep, gram_send, w_keep, w_send1, w_send2, w_send3,
                   table_high, table_low, gram_hh, gram_hl, weights):
    units = own_ref.shape[0]
    half = units // 2
    tile = part_a.shape[0]
    blocks = tile // BLOCK_STARS
    y, c = place[3], place[2]
    gram_hh[...] = jnp.zeros_like(gram_hh)
    gram_hl[...] = jnp.zeros_like(gram_hl)
    weights[...] = jnp.zeros_like(weights)

    def put(start, value):
        high, low = split_low(value)
        rows = pl.ds(pl.multiple_of(start, 128), value.shape[0])
        table_high[rows, :] = high
        table_low[rows, :] = low

    put(y * units, own_ref[...])
    for k in range(3):
        base = lax.rem(y + 3 - k, 4) * units
        put(base + c * half, half_ref[k * half:(k + 1) * half, :])
        put(base + (1 - c) * half, other_ref[k * half:(k + 1) * half, :])

    for i, part_ref in enumerate((part_a, part_b)):
        for block in range(blocks):
            rows = pl.ds(i * tile + block * BLOCK_STARS, BLOCK_STARS)
            groups = [uses[use, i * blocks + block] for use in range(USES)]
            starts = [pl.multiple_of(g * GROUP, GROUP) for g in groups]
            load = load_ref[rows, :]
            high_table = jnp.concatenate([table_high[pl.ds(s, GROUP), :] for s in starts], axis=0)
            low_table = jnp.concatenate([table_low[pl.ds(s, GROUP), :] for s in starts], axis=0)
            offset = jnp.dot(load, high_table, preferred_element_type=F32)
            offset = offset + jnp.dot(load, low_table, preferred_element_type=F32)
            high, low = split_low(part_ref[pl.ds(block * BLOCK_STARS, BLOCK_STARS), :] - offset)
            high_ref[rows, :] = high
            low_ref[rows, :] = low
            product = dot_rows(load, high)
            for use in range(USES):
                weights[pl.ds(starts[use], GROUP), :] += product[use * GROUP:(use + 1) * GROUP, :]
        rows = pl.ds(i * tile, tile)
        gram_hh[...] += dot_rows(high_ref[rows, :], high_ref[rows, :])
        gram_hl[...] += dot_rows(high_ref[rows, :], low_ref[rows, :])
    cross = gram_hl[...]
    gram = gram_hh[...] + cross + cross.T
    packed = jnp.concatenate([gram[:128, :128], gram[128:, :128], gram[128:, 128:]], axis=0)
    zero = jnp.concatenate([packed[:96], packed[96:192]], axis=1)
    one = jnp.concatenate([packed[192:288], packed[288:]], axis=1)
    first = c == 0
    gram_keep[...] = jnp.where(first, zero, one)
    gram_send[...] = jnp.where(first, one, zero)
    w_keep[...] = weights[pl.ds(pl.multiple_of(y * units, 256), units), :]
    for k, ref in enumerate((w_send1, w_send2, w_send3)):
        base = lax.rem(y + k + 1, 4) * units
        ref[...] = weights[pl.ds(pl.multiple_of(base, 256), units), :].astype(BF16)


def raw_kernel(tile, res_ref, high_ref, out_ref):
    def body(i, carry):
        columns = pl.ds(pl.multiple_of(i * tile, tile), tile)
        out_ref[:, columns] = dot_rows(high_ref[...], res_ref[:, columns])
        return carry

    lax.fori_loop(0, res_ref.shape[1] // tile, body, 0)


def finish_kernel(place, raw_ref, zero_ref, w_keep, w1, w2, w3, keep_ref, send_ref, ordered):
    weights = w_keep[...] + w1[...].astype(F32) + w2[...].astype(F32) + w3[...].astype(F32)
    total = raw_ref[...] - dot_rows(weights.astype(BF16), zero_ref[...])
    bins = total.T
    for chip in range(16):
        for core in range(2):
            source = (chip * 2 + core) * 64
            target = (core * 16 + chip) * 64
            ordered[target:target + 64, :] = bins[source:source + 64, :]
    half = keep_ref.shape[0]
    c = place[2]
    keep_ref[...] = ordered[pl.ds(pl.multiple_of(c * half, half), half), :]
    send_ref[...] = ordered[pl.ds(pl.multiple_of((1 - c) * half, half), half), :].astype(BF16)


def quarters(me, total, kind):
    rows = total.shape[0] // 4
    pieces = [
        lax.dynamic_slice_in_dim(total, lax.rem(me + k, 4) * rows, rows, 0) for k in range(4)
    ]
    return pieces[0], [p.astype(kind) for p in pieces[1:]]


def add_four(own, got):
    return (own + got[1]) + (got[0] + got[2])


def invert_factor(matrix, out_ref, panel=8):
    lanes, tiles = 128, 16
    row_in_tile = lax.broadcasted_iota(jnp.int32, (8, lanes), 0)
    rows = lax.broadcasted_iota(jnp.int32, (lanes, lanes), 0)
    unit = (rows == lax.broadcasted_iota(jnp.int32, (lanes, lanes), 1)).astype(F32)
    work = [matrix[8 * i:8 * i + 8, :] for i in range(tiles)]
    inverse = [unit[8 * i:8 * i + 8, :] for i in range(tiles)]

    def spread(value):
        return jnp.broadcast_to(value, (8, lanes))

    for j in range(0, lanes, panel):
        tile, at = divmod(j, 8)
        top = [spread(work[tile][at + k:at + k + 1, :]) for k in range(panel)]
        low = [spread(inverse[tile][at + k:at + k + 1, :]) for k in range(panel)]
        entry = {
            (p, q): spread(top[p][:, j + q:j + q + 1])
            for p in range(panel) for q in range(p, panel)
        }
        top_solved, low_solved, factors = {}, {}, {}
        for k in range(0, panel, 2):
            a, b, d = entry[k, k], entry[k, k + 1], entry[k + 1, k + 1]
            det = a * d - b * b
            scale = 1.0 / det
            i00, i01, i11 = d * scale, b * scale, a * scale
            root = lax.rsqrt(a)
            r = at + k
            out_ref[j + k:j + k + 1, :] = (low[k] * root)[r:r + 1, :]
            under = (a * low[k + 1] - b * low[k]) * (root * lax.rsqrt(det))
            out_ref[j + k + 1:j + k + 2, :] = under[r + 1:r + 2, :]
            for rows_of, solved in ((top, top_solved), (low, low_solved)):
                solved[k] = i00 * rows_of[k] - i01 * rows_of[k + 1]
                solved[k + 1] = i11 * rows_of[k + 1] - i01 * rows_of[k]
            for q in range(k + 2, panel):
                u, v = entry[k, q], entry[k + 1, q]
                factors[k, q], factors[k + 1, q] = i00 * u - i01 * v, i11 * v - i01 * u
            for p in range(k + 2, panel):
                for q in range(p, panel):
                    entry[p, q] = entry[p, q] - (entry[k, p] * factors[k, q] + entry[k + 1, p] * factors[k + 1, q])
                for rows_of in (top, low):
                    rows_of[p] = rows_of[p] - (factors[k, p] * rows_of[k] + factors[k + 1, p] * rows_of[k + 1])
        for solved in (top_solved, low_solved):
            for k in range(panel - 3, -1, -1):
                for q in range(panel - 1, k // 2 * 2 + 1, -1):
                    solved[k] = solved[k] - factors[k, q] * solved[q]
        top_rows = [top_solved[k] for k in range(panel)]
        low_rows = [low_solved[k] for k in range(panel)]
        for i in range(tile, tiles):
            if i == tile and at + panel == 8:
                continue
            columns = [spread(work[i][:, j + k:j + k + 1]) for k in range(panel)]
            if i == tile:
                columns = [jnp.where(row_in_tile >= at + panel, m, 0.0) for m in columns]
            work[i] = work[i] - sum_pairs([m * t for m, t in zip(columns, top_rows)])
            inverse[i] = inverse[i] - sum_pairs([m * t for m, t in zip(columns, low_rows)])


def sum_pairs(terms):
    while len(terms) > 1:
        terms = [a + b for a, b in zip(terms[::2], terms[1::2])]
    return terms[0]


def dot_plain(a, b):
    return jnp.dot(a, b, preferred_element_type=F32, precision=HIGHEST)


def dot_plain(a, b):
    return jnp.dot(a, b, preferred_element_type=F32, precision=HIGHEST)


def factor_kernel(place, mine_ref, other_ref, inverse_ref, inv_high, inv_low, top, bottom):
    first = place[2] == 0
    mine, other = mine_ref[...] * (1.0 / STARS), other_ref[...] * (1.0 / STARS)
    zero, one = jnp.where(first, mine, other), jnp.where(first, other, mine)
    packed = jnp.concatenate([zero[:, :128], zero[:, 128:], one[:, :128], one[:, 128:]], axis=0)
    invert_factor(packed[:128], top)
    upper = top[...]
    lower = dot_last(packed[128:256], upper, HIGHEST)
    invert_factor(packed[256:] - dot_last(lower, lower, HIGHEST), bottom)
    corner = bottom[...]
    left = -dot_plain(corner, dot_plain(lower, upper))
    inverse_ref[:128, :128] = upper
    inverse_ref[:128, 128:] = jnp.zeros_like(upper)
    inverse_ref[128:, :128] = left
    inverse_ref[128:, 128:] = corner
    high, low = split_low(inverse_ref[...])
    inv_high[...] = high
    inv_low[...] = low


def basis_kernel(tiles, high_ref, low_ref, inv_high, inv_low, out_ref, buffer, sems):
    tile = high_ref.shape[0] // tiles
    copies = []
    for i in range(tiles):
        rows = pl.ds(i * tile, tile)
        buffer[rows, :] = (
            dot_last(high_ref[rows, :], inv_high[...])
            + dot_last(high_ref[rows, :], inv_low[...])
            + dot_last(low_ref[rows, :], inv_high[...])
        )
        copy = pltpu.make_async_copy(buffer.at[rows, :], out_ref.at[rows, :], sems.at[i])
        copy.start()
        copies.append(copy)
    for copy in copies:
        copy.wait()


def modes_kernel(kept, got1, got2, got3, inverse_ref, out_ref):
    raw = (kept[...] + got1[...] + got2[...] + got3[...]) * (1.0 / STARS)
    out_ref[...] = dot_last(raw, inverse_ref[...], HIGHEST)


def on_device(residuals, loadings, zero_points, sketch_matrix, use_lists):
    rows, bins = residuals.shape
    units = zero_points.shape[0]
    r = lax.axis_index("rows")
    x, z, c, y = r // 8, (r // 2) % 4, r % 2, lax.axis_index("units")
    place = jnp.stack([x, z, c, y]).astype(jnp.int32)
    square = (MODES, MODES)
    own, half, sketch_near = resident(
        project_kernel, [place], [],
        [on_chip((units, MODES)), on_chip((units // 2, MODES)), on_chip((bins, MODES), BF16)],
        [pltpu.VMEM((units, bins), BF16), pltpu.SemaphoreType.DMA((2,))],
        flops=2 * units * bins * MODES, far=[zero_points, sketch_matrix],
    )
    shifted = shift_all("y", [half] * 3)
    part_a, near = resident(
        fetch_kernel, [], [sketch_near],
        [on_chip((rows // 2, MODES)), on_chip((rows, bins), BF16)],
        [pltpu.SemaphoreType.DMA((2,))], flops=rows * bins * MODES, far=[residuals],
    )
    halves = jnp.concatenate(shifted, axis=0)
    others = send(halves, SWAP)
    part_b, = resident(
        sketch_rest_kernel, [], [sketch_near, near],
        [on_chip((rows // 2, MODES))], flops=rows * bins * MODES,
    )
    high, low, gram_keep, gram_send, w_keep, *w_sends = resident(
        correct_kernel, [place, use_lists.T],
        [part_a, part_b, loadings, own, halves, others],
        [on_chip((rows, MODES), BF16)] * 2 + [on_chip((96, MODES))] * 2 + [on_chip((units, MODES))]
        + [on_chip((units, MODES), BF16)] * 3,
        [
            pltpu.VMEM((4 * units, MODES), BF16),
            pltpu.VMEM((4 * units, MODES), BF16),
            pltpu.VMEM(square, F32),
            pltpu.VMEM(square, F32),
            pltpu.VMEM((4 * units, MODES), F32),
        ],
        flops=2 * rows * bins * MODES,
    )
    w_got = shift_all("y", w_sends)
    gram = gram_keep + send(gram_send, SWAP)
    raw, = resident(
        functools.partial(raw_kernel, 512), [], [near, high],
        [on_chip((MODES, bins))], flops=2 * rows * bins * MODES,
    )
    for axis in "xzy":
        for pairs in PAIRS[axis]:
            gram = gram + send(gram, pairs)
    gram_other = send(gram, SWAP)
    keep, sent = resident(
        finish_kernel, [place], [raw, zero_points, w_keep, *w_got],
        [on_chip((bins // 2, MODES)), on_chip((bins // 2, MODES), BF16)],
        [pltpu.VMEM((bins, MODES), F32)], flops=2 * units * bins * MODES,
    )
    arrived = send(sent, SWAP)
    keep, sends = quarters(x, keep + arrived.astype(F32), BF16)
    keep, *sends = lax.optimization_barrier((keep, *sends))
    keep, sends = quarters(z, add_four(keep, [g.astype(F32) for g in shift_all("x", sends)]), F32)
    keep, sends = quarters(y, add_four(keep, shift_all("z", sends)), F32)
    raw_got = shift_all("y", sends)
    inverse, inv_high, inv_low = resident(
        factor_kernel, [place], [gram, gram_other],
        [on_chip(square), on_chip(square, BF16), on_chip(square, BF16)],
        [pltpu.VMEM((128, 128), F32)] * 2, flops=1 << 33,
    )
    star_basis, = resident(
        functools.partial(basis_kernel, 4), [], [high, low, inv_high, inv_low],
        [jax.ShapeDtypeStruct((rows, MODES), F32)],
        [pltpu.VMEM((rows, MODES), F32), pltpu.SemaphoreType.DMA((4,))],
        flops=6 * rows * MODES * MODES, out_specs=[pl.BlockSpec(memory_space=pltpu.HBM)],
    )
    bin_modes, = resident(
        modes_kernel, [], [keep, *raw_got, inverse],
        [jax.ShapeDtypeStruct((keep.shape[0], MODES), F32)], flops=1 << 28,
    )
    return (star_basis, bin_modes)


def solution(mesh):
    in_specs = (
        P(("rows", "units"), None),
        P(("rows", "units"), None),
        P("units", None),
        P(),
        P(("rows", "units"), None),
    )
    out_specs = (P(("rows", "units"), None), P(("rows", "units"), None))
    return jax.shard_map(on_device, mesh=mesh, in_specs=in_specs, out_specs=out_specs, check_vma=False)
```

```python
import functools

import jax
import jax.numpy as jnp
from jax import lax
from jax.experimental import pallas as pl
from jax.experimental.pallas import tpu as pltpu
from jax.sharding import PartitionSpec as P


GROUP = 64
USES = 4
BLOCK_STARS = 128
MODES = 256
STARS = 524288
AXES = ("rows", "units")
F32 = jnp.float32
BF16 = jnp.bfloat16
HIGHEST = lax.Precision.HIGHEST


def split_low(value):
    high = value.astype(BF16)
    return high, (value - high.astype(F32)).astype(BF16)


def dot_rows(a, b):
    return lax.dot_general(a, b, (((0,), (0,)), ((), ())), preferred_element_type=F32)


def dot_last(a, b, precision=None):
    return lax.dot_general(
        a, b, (((1,), (1,)), ((), ())), preferred_element_type=F32, precision=precision
    )


def permutation(move):
    pairs = []
    for x in range(4):
        for z in range(4):
            for c in range(2):
                for y in range(4):
                    u, w, d, v = move(x, z, c, y)
                    pairs.append((((x * 4 + z) * 2 + c) * 4 + y, ((u * 4 + w) * 2 + d) * 4 + v))
    return pairs


SWAP = permutation(lambda x, z, c, y: (x, z, 1 - c, y))
SHIFTS = {
    "x": [permutation(lambda x, z, c, y, k=k: ((x + k) % 4, z, c, y)) for k in (1, 2, 3)],
    "y": [permutation(lambda x, z, c, y, k=k: (x, z, c, (y + k) % 4)) for k in (1, 2, 3)],
    "z": [permutation(lambda x, z, c, y, k=k: (x, (z + k) % 4, c, y)) for k in (1, 2, 3)],
}

PAIRS = {
    "x": [permutation(lambda x, z, c, y: (x ^ 1, z, c, y)), permutation(lambda x, z, c, y: (3 - x, z, c, y))],
    "y": [permutation(lambda x, z, c, y: (x, z, c, y ^ 1)), permutation(lambda x, z, c, y: (x, z, c, 3 - y))],
    "z": [permutation(lambda x, z, c, y: (x, z ^ 1, c, y)), permutation(lambda x, z, c, y: (x, 3 - z, c, y))],
}


def send(value, pairs):
    return lax.ppermute(value, AXES, pairs)


def shift_all(axis, pieces):
    return [send(p, SHIFTS[axis][k]) for k, p in enumerate(pieces)]


def on_chip(shape, kind=F32):
    return pltpu.VMEM(shape, kind)


def resident(kernel, scalars, arrays, outs, scratch=(), flops=0, limit=16, out_specs=None, far=()):
    vmem = pl.BlockSpec(memory_space=pltpu.VMEM)
    smem = pl.BlockSpec(memory_space=pltpu.SMEM)
    arrays = [pltpu.with_memory_space_constraint(a, pltpu.VMEM) for a in arrays]
    far = [pltpu.with_memory_space_constraint(a, pltpu.HBM) for a in far]
    return pl.pallas_call(
        kernel,
        in_specs=[smem] * len(scalars) + [vmem] * len(arrays) + [pl.BlockSpec(memory_space=pltpu.HBM)] * len(far),
        out_specs=out_specs or [vmem] * len(outs),
        out_shape=list(outs),
        scratch_shapes=list(scratch),
        compiler_params=pltpu.CompilerParams(vmem_limit_bytes=limit << 20),
        cost_estimate=pl.CostEstimate(flops=flops, bytes_accessed=1 << 16, transcendentals=0),
    )(*scalars, *arrays, *far)


def project_kernel(place, zero_hbm, sketch_hbm, full_ref, half_ref, sketch, zero, sems):
    copies = [
        pltpu.make_async_copy(zero_hbm, zero, sems.at[0]),
        pltpu.make_async_copy(sketch_hbm, sketch, sems.at[1]),
    ]
    for copy in copies:
        copy.start()
    for copy in copies:
        copy.wait()
    full_ref[...] = jnp.dot(zero[...], sketch[...], preferred_element_type=F32)
    half = full_ref.shape[0] // 2
    half_ref[...] = full_ref[pl.ds(pl.multiple_of(place[2] * half, half), half), :]


def fetch_kernel(sketch_ref, res_hbm, out_ref, res_ref, sems):
    half = out_ref.shape[0]
    copies = []
    for i in range(2):
        rows = pl.ds(i * half, half)
        copies.append(pltpu.make_async_copy(res_hbm.at[rows, :], res_ref.at[rows, :], sems.at[i]))
        copies[i].start()
    copies[0].wait()
    sketch_kernel(sketch_ref, res_ref, out_ref, 0)
    copies[1].wait()


def sketch_kernel(sketch_ref, res_ref, out_ref, first):
    tile = out_ref.shape[0] // 2
    for i in range(2):
        rows = pl.ds(i * tile, tile)
        out_ref[rows, :] = jnp.dot(
            res_ref[pl.ds(first + i * tile, tile), :], sketch_ref[...], preferred_element_type=F32
        )


def sketch_rest_kernel(sketch_ref, res_ref, out_ref):
    sketch_kernel(sketch_ref, res_ref, out_ref, res_ref.shape[0] // 2)


def correct_kernel(place, uses, part_a, part_b, load_ref, own_ref, half_ref, other_ref,
                   high_ref, low_ref, gram_keep, gram_send, w_keep, w_send1, w_send2, w_send3,
                   table_high, table_low, gram_hh, gram_hl, weights):
    units = own_ref.shape[0]
    half = units // 2
    tile = part_a.shape[0]
    blocks = tile // BLOCK_STARS
    y, c = place[3], place[2]
    gram_hh[...] = jnp.zeros_like(gram_hh)
    gram_hl[...] = jnp.zeros_like(gram_hl)
    weights[...] = jnp.zeros_like(weights)

    def put(start, value):
        high, low = split_low(value)
        rows = pl.ds(pl.multiple_of(start, 128), value.shape[0])
        table_high[rows, :] = high
        table_low[rows, :] = low

    put(y * units, own_ref[...])
    for k in range(3):
        base = lax.rem(y + 3 - k, 4) * units
        put(base + c * half, half_ref[k * half:(k + 1) * half, :])
        put(base + (1 - c) * half, other_ref[k * half:(k + 1) * half, :])

    for i, part_ref in enumerate((part_a, part_b)):
        for block in range(blocks):
            rows = pl.ds(i * tile + block * BLOCK_STARS, BLOCK_STARS)
            groups = [uses[use, i * blocks + block] for use in range(USES)]
            starts = [pl.multiple_of(g * GROUP, GROUP) for g in groups]
            load = load_ref[rows, :]
            high_table = jnp.concatenate([table_high[pl.ds(s, GROUP), :] for s in starts], axis=0)
            low_table = jnp.concatenate([table_low[pl.ds(s, GROUP), :] for s in starts], axis=0)
            offset = jnp.dot(load, high_table, preferred_element_type=F32)
            offset = offset + jnp.dot(load, low_table, preferred_element_type=F32)
            high, low = split_low(part_ref[pl.ds(block * BLOCK_STARS, BLOCK_STARS), :] - offset)
            high_ref[rows, :] = high
            low_ref[rows, :] = low
            product = dot_rows(load, high)
            for use in range(USES):
                weights[pl.ds(starts[use], GROUP), :] += product[use * GROUP:(use + 1) * GROUP, :]
        rows = pl.ds(i * tile, tile)
        gram_hh[...] += dot_rows(high_ref[rows, :], high_ref[rows, :])
        gram_hl[...] += dot_rows(high_ref[rows, :], low_ref[rows, :])
    cross = gram_hl[...]
    gram = gram_hh[...] + cross + cross.T
    left = lax.broadcasted_iota(jnp.int32, (64, 128), 1) < 64
    upper, lower = gram[:128, :128], gram[128:, 128:]
    packed = jnp.concatenate(
        [
            gram[128:, :128],
            jnp.where(left, upper[:64], upper[64:]),
            jnp.where(left, lower[:64], lower[64:]),
            jnp.where(left, upper[64:], lower[:64]),
        ],
        axis=0,
    )
    zero = jnp.concatenate([packed[:80], packed[80:160]], axis=1)
    one = jnp.concatenate([packed[160:240], packed[240:]], axis=1)
    first = c == 0
    gram_keep[...] = jnp.where(first, zero, one)
    gram_send[...] = jnp.where(first, one, zero)
    w_keep[...] = weights[pl.ds(pl.multiple_of(y * units, 256), units), :]
    for k, ref in enumerate((w_send1, w_send2, w_send3)):
        base = lax.rem(y + k + 1, 4) * units
        ref[...] = weights[pl.ds(pl.multiple_of(base, 256), units), :].astype(BF16)


def raw_kernel(first, res_ref, high_ref, out_ref):
    tile = out_ref.shape[1] // 2
    for i in range(2):
        columns = pl.ds(first + i * tile, tile)
        out_ref[:, i * tile:(i + 1) * tile] = dot_rows(high_ref[...], res_ref[:, columns])


def finish_kernel(place, raw_a, raw_b, zero_ref, w_keep, w1, w2, w3, keep_ref, send_ref, ordered):
    weights = w_keep[...] + w1[...].astype(F32) + w2[...].astype(F32) + w3[...].astype(F32)
    raw = jnp.concatenate([raw_a[...], raw_b[...]], axis=1)
    total = raw - dot_rows(weights.astype(BF16), zero_ref[...])
    bins = total.T
    for chip in range(16):
        for core in range(2):
            source = (chip * 2 + core) * 64
            target = (core * 16 + chip) * 64
            ordered[target:target + 64, :] = bins[source:source + 64, :]
    half = keep_ref.shape[0]
    c = place[2]
    keep_ref[...] = ordered[pl.ds(pl.multiple_of(c * half, half), half), :]
    send_ref[...] = ordered[pl.ds(pl.multiple_of((1 - c) * half, half), half), :].astype(BF16)


def quarters(me, total, kind):
    rows = total.shape[0] // 4
    pieces = [
        lax.dynamic_slice_in_dim(total, lax.rem(me + k, 4) * rows, rows, 0) for k in range(4)
    ]
    return pieces[0], [p.astype(kind) for p in pieces[1:]]


def add_four(own, got):
    return (own + got[1]) + (got[0] + got[2])


def invert_factor(matrix, out_ref, panel=8):
    lanes, tiles = 128, 16
    row_in_tile = lax.broadcasted_iota(jnp.int32, (8, lanes), 0)
    rows = lax.broadcasted_iota(jnp.int32, (lanes, lanes), 0)
    unit = (rows == lax.broadcasted_iota(jnp.int32, (lanes, lanes), 1)).astype(F32)
    work = [matrix[8 * i:8 * i + 8, :] for i in range(tiles)]
    inverse = [unit[8 * i:8 * i + 8, :] for i in range(tiles)]

    def spread(value):
        return jnp.broadcast_to(value, (8, lanes))

    for j in range(0, lanes, panel):
        tile, at = divmod(j, 8)
        top = [spread(work[tile][at + k:at + k + 1, :]) for k in range(panel)]
        low = [spread(inverse[tile][at + k:at + k + 1, :]) for k in range(panel)]
        entry = {
            (p, q): spread(top[p][:, j + q:j + q + 1])
            for p in range(panel) for q in range(p, panel)
        }
        top_solved, low_solved, factors = {}, {}, {}
        for k in range(0, panel, 2):
            a, b, d = entry[k, k], entry[k, k + 1], entry[k + 1, k + 1]
            det = a * d - b * b
            scale = 1.0 / det
            i00, i01, i11 = d * scale, b * scale, a * scale
            root = lax.rsqrt(a)
            r = at + k
            out_ref[j + k:j + k + 1, :] = (low[k] * root)[r:r + 1, :]
            under = (a * low[k + 1] - b * low[k]) * (root * lax.rsqrt(det))
            out_ref[j + k + 1:j + k + 2, :] = under[r + 1:r + 2, :]
            for rows_of, solved in ((top, top_solved), (low, low_solved)):
                solved[k] = i00 * rows_of[k] - i01 * rows_of[k + 1]
                solved[k + 1] = i11 * rows_of[k + 1] - i01 * rows_of[k]
            for q in range(k + 2, panel):
                u, v = entry[k, q], entry[k + 1, q]
                factors[k, q], factors[k + 1, q] = i00 * u - i01 * v, i11 * v - i01 * u
            for p in range(k + 2, panel):
                for q in range(p, panel):
                    entry[p, q] = entry[p, q] - (entry[k, p] * factors[k, q] + entry[k + 1, p] * factors[k + 1, q])
                for rows_of in (top, low):
                    rows_of[p] = rows_of[p] - (factors[k, p] * rows_of[k] + factors[k + 1, p] * rows_of[k + 1])
        for solved in (top_solved, low_solved):
            for k in range(panel - 3, -1, -1):
                for q in range(panel - 1, k // 2 * 2 + 1, -1):
                    solved[k] = solved[k] - factors[k, q] * solved[q]
        top_rows = [top_solved[k] for k in range(panel)]
        low_rows = [low_solved[k] for k in range(panel)]
        for i in range(tile, tiles):
            if i == tile and at + panel == 8:
                continue
            columns = [spread(work[i][:, j + k:j + k + 1]) for k in range(panel)]
            if i == tile:
                columns = [jnp.where(row_in_tile >= at + panel, m, 0.0) for m in columns]
            work[i] = work[i] - sum_pairs([m * t for m, t in zip(columns, top_rows)])
            inverse[i] = inverse[i] - sum_pairs([m * t for m, t in zip(columns, low_rows)])


def sum_pairs(terms):
    while len(terms) > 1:
        terms = [a + b for a, b in zip(terms[::2], terms[1::2])]
    return terms[0]


def dot_plain(a, b):
    return jnp.dot(a, b, preferred_element_type=F32, precision=HIGHEST)


def dot_plain(a, b):
    return jnp.dot(a, b, preferred_element_type=F32, precision=HIGHEST)


def factor_kernel(place, mine_ref, other_ref, inv_high, inv_low, inverse_ref, top, bottom):
    first = place[2] == 0
    mine, other = mine_ref[...] * (1.0 / STARS), other_ref[...] * (1.0 / STARS)
    zero, one = jnp.where(first, mine, other), jnp.where(first, other, mine)
    packed = jnp.concatenate([zero[:, :128], zero[:, 128:], one[:, :128], one[:, 128:]], axis=0)
    left = lax.broadcasted_iota(jnp.int32, (64, 128), 1) < 64
    upper_pairs, lower_pairs, corners = packed[128:192], packed[192:256], packed[256:]
    under = jnp.concatenate([upper_pairs, jnp.where(left, corners, upper_pairs)], axis=0)
    over = jnp.concatenate([jnp.where(left, lower_pairs, corners), lower_pairs], axis=0)
    rows = lax.broadcasted_iota(jnp.int32, (128, 128), 0)
    columns = lax.broadcasted_iota(jnp.int32, (128, 128), 1)
    invert_factor(jnp.where((rows < 64) & (columns >= 64), under.T, under), top)
    upper = top[...]
    lower = dot_last(packed[:128], upper, HIGHEST)
    second = jnp.where((rows >= 64) & (columns < 64), over.T, over)
    invert_factor(second - dot_last(lower, lower, HIGHEST), bottom)
    corner = bottom[...]
    left = -dot_plain(corner, dot_plain(lower, upper))
    inverse_ref[:128, :128] = upper
    inverse_ref[:128, 128:] = jnp.zeros_like(upper)
    inverse_ref[128:, :128] = left
    inverse_ref[128:, 128:] = corner
    high, low = split_low(inverse_ref[...])
    inv_high[...] = high
    inv_low[...] = low


def basis_kernel(tiles, high_ref, low_ref, inv_high, inv_low, out_ref, buffer, sems):
    tile = high_ref.shape[0] // tiles
    copies = []
    for i in range(tiles):
        rows = pl.ds(i * tile, tile)
        buffer[rows, :] = (
            dot_last(high_ref[rows, :], inv_high[...])
            + dot_last(high_ref[rows, :], inv_low[...])
            + dot_last(low_ref[rows, :], inv_high[...])
        )
        copy = pltpu.make_async_copy(buffer.at[rows, :], out_ref.at[rows, :], sems.at[i])
        copy.start()
        copies.append(copy)
    for copy in copies:
        copy.wait()


def modes_kernel(kept, got1, got2, got3, inv_high, inv_low, out_ref):
    high, low = split_low((kept[...] + got1[...] + got2[...] + got3[...]) * (1.0 / STARS))
    out_ref[...] = (
        dot_last(high, inv_high[...]) + dot_last(high, inv_low[...]) + dot_last(low, inv_high[...])
    )


def on_device(residuals, loadings, zero_points, sketch_matrix, use_lists):
    rows, bins = residuals.shape
    units = zero_points.shape[0]
    r = lax.axis_index("rows")
    x, z, c, y = r // 8, (r // 2) % 4, r % 2, lax.axis_index("units")
    place = jnp.stack([x, z, c, y]).astype(jnp.int32)
    square = (MODES, MODES)
    own, half, sketch_near = resident(
        project_kernel, [place], [],
        [on_chip((units, MODES)), on_chip((units // 2, MODES)), on_chip((bins, MODES), BF16)],
        [pltpu.VMEM((units, bins), BF16), pltpu.SemaphoreType.DMA((2,))],
        flops=2 * units * bins * MODES, far=[zero_points, sketch_matrix],
    )
    shifted = shift_all("y", [half] * 3)
    part_a, near = resident(
        fetch_kernel, [], [sketch_near],
        [on_chip((rows // 2, MODES)), on_chip((rows, bins), BF16)],
        [pltpu.SemaphoreType.DMA((2,))], flops=rows * bins * MODES, far=[residuals],
    )
    halves = jnp.concatenate(shifted, axis=0)
    others = send(halves, SWAP)
    part_b, = resident(
        sketch_rest_kernel, [], [sketch_near, near],
        [on_chip((rows // 2, MODES))], flops=rows * bins * MODES,
    )
    high, low, gram_keep, gram_send, w_keep, *w_sends = resident(
        correct_kernel, [place, use_lists.T],
        [part_a, part_b, loadings, own, halves, others],
        [on_chip((rows, MODES), BF16)] * 2 + [on_chip((80, MODES))] * 2 + [on_chip((units, MODES))]
        + [on_chip((units, MODES), BF16)] * 3,
        [
            pltpu.VMEM((4 * units, MODES), BF16),
            pltpu.VMEM((4 * units, MODES), BF16),
            pltpu.VMEM(square, F32),
            pltpu.VMEM(square, F32),
            pltpu.VMEM((4 * units, MODES), F32),
        ],
        flops=2 * rows * bins * MODES,
    )
    w_got = shift_all("y", w_sends)
    gram = gram_keep + send(gram_send, SWAP)
    raws = [
        resident(
            functools.partial(raw_kernel, i * (bins // 2)), [], [near, high],
            [on_chip((MODES, bins // 2))], flops=rows * bins * MODES,
        )[0]
        for i in range(2)
    ]
    for axis in "xzy":
        for pairs in PAIRS[axis]:
            gram = gram + send(gram, pairs)
    gram_other = send(gram, SWAP)
    keep, sent = resident(
        finish_kernel, [place], [*raws, zero_points, w_keep, *w_got],
        [on_chip((bins // 2, MODES)), on_chip((bins // 2, MODES), BF16)],
        [pltpu.VMEM((bins, MODES), F32)], flops=2 * units * bins * MODES,
    )
    arrived = send(sent, SWAP)
    keep, sends = quarters(x, keep + arrived.astype(F32), BF16)
    keep, *sends = lax.optimization_barrier((keep, *sends))
    keep, sends = quarters(z, add_four(keep, [g.astype(F32) for g in shift_all("x", sends)]), F32)
    keep, sends = quarters(y, add_four(keep, shift_all("z", sends)), F32)
    raw_got = shift_all("y", sends)
    inv_high, inv_low = resident(
        factor_kernel, [place], [gram, gram_other],
        [on_chip(square, BF16)] * 2,
        [pltpu.VMEM(square, F32)] + [pltpu.VMEM((128, 128), F32)] * 2, flops=1 << 33,
    )
    star_basis, = resident(
        functools.partial(basis_kernel, 8), [], [high, low, inv_high, inv_low],
        [jax.ShapeDtypeStruct((rows, MODES), F32)],
        [pltpu.VMEM((rows, MODES), F32), pltpu.SemaphoreType.DMA((8,))],
        flops=6 * rows * MODES * MODES, out_specs=[pl.BlockSpec(memory_space=pltpu.HBM)],
    )
    bin_modes, = resident(
        modes_kernel, [], [keep, *raw_got, inv_high, inv_low],
        [jax.ShapeDtypeStruct((keep.shape[0], MODES), F32)], flops=1 << 28,
    )
    return (star_basis, bin_modes)


def solution(mesh):
    in_specs = (
        P(("rows", "units"), None),
        P(("rows", "units"), None),
        P("units", None),
        P(),
        P(("rows", "units"), None),
    )
    out_specs = (P(("rows", "units"), None), P(("rows", "units"), None))
    return jax.shard_map(
        on_device, mesh=mesh, in_specs=in_specs, out_specs=out_specs, check_vma=False
    )
```
